256 devices in a mesh: track: 16 (over z, x_lo), tm: 16 (over x_hi, y, core).
Axes of the slice: x: 4 (x_hi: 2, x_lo: 2; x = x_hi * 2 + x_lo), y: 4, z: 8, core: 2. Of those that a mesh axis runs over, the one named last changes fastest.
Arguments:
- positions: float32 [3, 32, 6144], P(None, 'tm', 'track'), may hold values from -6 to 6
- embeddings: float32 [32, 128, 6144], P('tm', None, 'track'), may hold values from -6 to 6
- visible: int32 [32, 6144], P('tm', 'track'), may hold values 0 or 1
Outputs:
- grad_positions: float32 [3, 32, 6144], P(None, 'tm', 'track')
- grad_embeddings: float32 [32, 128, 6144], P('tm', None, 'track')
- mean_loss: float32 [], replicated
The draws below stay inside these ranges and needn't reach their ends.
All inputs are finite; a program needn't handle non-finite values. No bound on the sum of `visible` on one device may be relied on, other than what follows from the above.
Results may differ from the reference program's by a relative error of at most 0.00014.
Values sent between devices are 32-bit elements; how exact they have to be, the bound alone decides.
A program may use at most 128 MiB of HBM per device.

```python
import math
import jax
import jax.numpy as jnp
from jax import lax

EMB = 128
TRACKS = 6144
FRAMES = 32


def place_ends(entries, own_key, low, largest):
    spot = [jax.random.randint(jax.random.fold_in(own_key, axis), (), 0, length) for axis, length in enumerate(entries.shape)]
    widest = entries.shape.index(max(entries.shape))
    next_to = spot[:widest] + [(spot[widest] + 1) % entries.shape[widest]] + spot[widest + 1:]
    return entries.at[tuple(spot)].set(low).at[tuple(next_to)].set(largest)


def level_of(stream_key, extent, pieces, least, largest):
    gain = 1.0
    for axis_at, blocks in pieces:
        draws = jax.random.uniform(jax.random.fold_in(jax.random.fold_in(stream_key, 6), axis_at), (blocks,), jnp.float32, least / len(pieces), largest / len(pieces))
        gain = gain * jnp.repeat(jnp.exp(draws), extent[axis_at] // blocks).reshape((-1,) + (1,) * (len(extent) - 1 - axis_at))
    return gain


def normal_values(rng, dims, scale, reach, split=(), dtype=jnp.bfloat16):
    drawn = scale * jax.random.normal(rng, dims, jnp.float32)
    if split:
        drawn = drawn * level_of(rng, dims, split, -0.22, 0.18)
    return jnp.clip(drawn, -reach, reach).astype(dtype)


def setup_inputs(seed: int = 0) -> dict:
    seeds = jax.random.split(jax.random.key(seed), 4)
    positions = normal_values(seeds[0], (3, FRAMES, TRACKS), 1.0, 6.0, ((1, 16), (2, 16)), jnp.float32)
    embeddings = normal_values(seeds[1], (FRAMES, EMB, TRACKS), 1.0, 6.0, ((0, 16), (2, 16)), jnp.float32)
    visible = place_ends((jax.random.randint(seeds[2], (FRAMES, TRACKS), 0, 4) < 3).astype(jnp.int32), jax.random.fold_in(seeds[2], 1), 0, 1)
    return {"positions": positions, "embeddings": embeddings, "visible": visible}


rigidity = 4.0
highest = lax.Precision.HIGHEST

def tile_terms(pos_a, mask_a, emb_a, pos_b, mask_b, emb_b, weight_scale):
    inv_root = 1.0 / math.sqrt(emb_a.shape[1])
    offset = pos_a[:, :, :, None] - pos_b[:, :, None, :]
    distance = jnp.sqrt(lax.optimization_barrier(jnp.sum(offset * offset, axis=0)) + 1.0)
    change = distance[1:] - distance[:-1]
    both_seen = mask_a[:, :, None] * mask_b[:, None, :]
    seen_pair = both_seen[1:] * both_seen[:-1]
    logits = jnp.einsum('fei,fej->fij', emb_a, emb_b, precision=highest) * inv_root
    affinity = jax.nn.sigmoid(logits)
    squared = seen_pair * change * change
    energy = jnp.sum(affinity * squared)
    grad_change = 2.0 * weight_scale * affinity * seen_pair * change
    padding = jnp.zeros_like(grad_change[:1])
    grad_dist = jnp.concatenate([padding, grad_change], 0) - jnp.concatenate([grad_change, padding], 0)
    scaled = (grad_dist / distance)[None] * offset
    grad_pos_a = lax.optimization_barrier(jnp.sum(scaled, axis=3))
    grad_pos_b = -lax.optimization_barrier(jnp.sum(scaled, axis=2))
    grad_logit = weight_scale * squared * affinity * (1.0 - affinity) * inv_root
    grad_emb_a = jnp.einsum('fij,fej->fei', grad_logit, emb_b, precision=highest)
    grad_emb_b = jnp.einsum('fij,fei->fej', grad_logit, emb_a, precision=highest)
    return (energy, grad_pos_a, grad_emb_a, grad_pos_b, grad_emb_b)

def reference(positions, embeddings, visible):
    frames = positions.shape[1]
    tracks = positions.shape[2]
    width = embeddings.shape[1]
    weight_scale = rigidity / math.sqrt(tracks)
    seen_mask = visible.astype(jnp.float32)
    tile_size = min(256, tracks)
    tile_count = tracks // tile_size
    pos_blocks = positions.reshape(3, frames, tile_count, tile_size).transpose(2, 0, 1, 3)
    mask_blocks = seen_mask.reshape(frames, tile_count, tile_size).transpose(1, 0, 2)
    emb_blocks = embeddings[:frames - 1].reshape(frames - 1, width, tile_count, tile_size).transpose(2, 0, 1, 3)

    def per_row(inputs):
        pos_a, mask_a, emb_a = inputs

        def advance(totals, others):
            pos_b, mask_b, emb_b = others
            energy, grad_pos_a, grad_emb_a, unused_pos, unused_emb = tile_terms(pos_a, mask_a, emb_a, pos_b, mask_b, emb_b, weight_scale)
            return ((totals[0] + energy, totals[1] + grad_pos_a, totals[2] + grad_emb_a), None)
        initial = (jnp.zeros((), jnp.float32), jnp.zeros_like(pos_a), jnp.zeros_like(emb_a))
        result, unused = lax.scan(advance, initial, (pos_blocks, mask_blocks, emb_blocks))
        return result
    energies, grad_pos, grad_emb = lax.map(per_row, (pos_blocks, mask_blocks, emb_blocks))
    grad_positions = grad_pos.transpose(1, 2, 0, 3).reshape(3, frames, tracks)
    grad_emb = grad_emb.transpose(1, 2, 0, 3).reshape(frames - 1, width, tracks)
    grad_embeddings = jnp.concatenate([grad_emb, jnp.zeros((1, width, tracks), jnp.float32)], 0)
    total = 0.5 * jnp.sum(energies)
    mean_loss = total / (tracks * (tracks - 1) / 2.0 * (frames - 1))
    return (grad_positions, grad_embeddings, mean_loss)
```

```python
import functools
import math

import jax
import jax.numpy as jnp
from jax import lax
from jax.experimental import pallas as pl
from jax.experimental.pallas import tpu as pltpu
from jax.sharding import PartitionSpec as P

f32, bf16 = jnp.float32, jnp.bfloat16
MESH = pl.DeviceIdType.MESH
rigidity = 4.0
HIDE = 2.0**20
LANE = 128
NBUF = 2

ROWS = 8
PLANES = 8
STEPS = 4


def owner(z, f):
    rel = lax.rem(z - 2 * f + 2 * ROWS, ROWS)
    upper = jnp.where((rel >= 1) & (rel <= 4), 1, 0)
    away = jnp.where(upper == 1, rel - 1, lax.rem(ROWS - rel, ROWS))
    other = jnp.where((away == 1) | (away == 2), 1, 0)
    slot = jnp.where(away >= 2, 1, 0)
    return 2 * f + upper, slot, other


def flip(core, other):
    return core + other - 2 * core * other


def split2(v):
    hi = v.astype(bf16)
    return hi, (v - hi.astype(f32)).astype(bf16)


def pieces(v):
    h = v.astype(bf16).astype(f32)
    m = (v - h).astype(bf16).astype(f32)
    return h, m, (v - h - m).astype(bf16).astype(f32)


def prep_cols(u, emb, width, buf, pc, mid, rhs, rd):
    for s in range(2):
        cs = slice(s * width, (s + 1) * width)
        hi, lo = split2(buf[u, s, 0:emb, :])
        rhs[u, 0:emb, cs] = hi
        rhs[u, emb : 2 * emb, cs] = lo
        rhs[u, 2 * emb : 3 * emb, cs] = hi
        q = buf[u, s, emb + 3 : emb + 4, :] * buf[u, s, emb + 11 : emb + 12, :]
        rows = lax.broadcasted_iota(jnp.int32, (LANE, width), 0)
        m = jnp.where(rows == 0, 1.0, 0.0) + jnp.where(rows == 1, (q - 1.0) * HIDE, 0.0)
        rhs[u, 3 * emb :, cs] = m.astype(bf16)
        for f in range(2):
            p = [
                buf[u, s, emb + 8 * f + c : emb + 8 * f + c + 1, :] - mid[8 * f + c : 8 * f + c + 1, 0:1]
                for c in range(3)
            ]
            out = []
            for c in range(3):
                pc[u, s, 8 * f + c : 8 * f + c + 1, :] = p[c]
                h, mm, l = pieces(p[c])
                out += [h, mm, h, mm, l, h]
            n = p[0] * p[0] + p[1] * p[1] + p[2] * p[2]
            one = jnp.ones_like(n)
            out += [one, one, one] + list(pieces(n)) + [jnp.zeros((8, width), f32)]
            rd[u, f, :, cs] = jnp.concatenate(out, 0).astype(bf16)


def prep_rows(valid, emb, width, buf, mid, ll, ld, tp):
    mean = (jnp.sum(buf[0, 0, emb:, :], 1, keepdims=True) + jnp.sum(buf[0, 1, emb:, :], 1, keepdims=True)) / (2.0 * width)
    mid[...] = jnp.broadcast_to(mean, mid.shape)
    for s in range(2):
        rs = slice(s * width, (s + 1) * width)
        hi, lo = split2(jnp.transpose(buf[0, s, 0:emb, :]) * (0.5 / math.sqrt(emb)))
        ll[rs, 0:emb] = hi
        ll[rs, emb : 2 * emb] = hi
        ll[rs, 2 * emb : 3 * emb] = lo
        q = buf[0, s, emb + 3 : emb + 4, :] * buf[0, s, emb + 11 : emb + 12, :] * valid
        one = jnp.ones_like(q)
        m = jnp.concatenate([(q - 1.0) * HIDE, one, jnp.zeros((LANE - 2, width), f32)], 0)
        ll[rs, 3 * emb :] = jnp.transpose(m).astype(bf16)
        for f in range(2):
            p = [
                buf[0, s, emb + 8 * f + c : emb + 8 * f + c + 1, :] - mid[8 * f + c : 8 * f + c + 1, 0:1]
                for c in range(3)
            ]
            out = []
            for c in range(3):
                h, mm, l = pieces(p[c])
                out += [-2.0 * h, -2.0 * h, -2.0 * mm, -2.0 * mm, -2.0 * h, -2.0 * l]
            n = p[0] * p[0] + p[1] * p[1] + p[2] * p[2] + 1.0
            out += list(pieces(n)) + [one, one, one, jnp.zeros((LANE - 24, width), f32)]
            ld[f, rs, :] = jnp.transpose(jnp.concatenate(out, 0)).astype(bf16)[:, 0:32]
            tp[f, rs, :] = jnp.transpose(jnp.concatenate(p + [jnp.zeros((LANE - 3, width), f32)], 0))


def dot_piece(k, n, u, r0, R, rhs, rd, ll, ld, sc):
    ns = slice(n, n + 256)
    if k == 0:
        sc[0][:, ns] = jnp.dot(ll[r0 : r0 + R, :], rhs[u, :, ns], preferred_element_type=f32)
    else:
        sc[k][:, ns] = jnp.dot(ld[k - 1, r0 : r0 + R, :], rd[u, k - 1, :, ns], preferred_element_type=f32)


def strip(s, u, r0, R, width, pc, acc, en, sc):
    xs, d0s, d1s, gs = sc
    A = [acc[k, r0 + s : r0 + s + 16, :] for k in range(8)]
    es = en[...]
    span = 256
    for c0 in range(0, 2 * width, span):
        cs = slice(c0, c0 + span)
        x, a0, a1 = xs[s : s + 16, cs], d0s[s : s + 16, cs], d1s[s : s + 16, cs]
        q0, q1 = lax.rsqrt(a0), lax.rsqrt(a1)
        ch = a1 * q1 - a0 * q0
        v = jnp.tanh(x) * ch
        h = ch + v
        g = h * (ch - v)
        hi = g.astype(bf16)
        gs[s : s + 16, cs] = hi
        gs[R + s : R + s + 16, cs] = (g - hi.astype(f32)).astype(bf16)
        e = h * ch
        w = (h * q0, h * q1)
        for k in range(0, span, LANE):
            j = c0 + k
            side, js = j // width, slice(j % width, j % width + LANE)
            for f in range(2):
                wk = w[f][:, k : k + LANE]
                A[4 * f] = A[4 * f] + wk
                for c in range(3):
                    A[4 * f + 1 + c] = A[4 * f + 1 + c] + wk * pc[u, side, 8 * f + c : 8 * f + c + 1, js]
            es = es + (e[0:8, k : k + LANE] + e[8:16, k : k + LANE])
    for k in range(8):
        acc[k, r0 + s : r0 + s + 16, :] = A[k]
    en[...] = es


def grad_dot(u, r0, R, emb, rhs, ge, sc):
    o = lax.dot_general(
        sc[3][...], rhs[u, 0 : 2 * emb, :], (((1,), (1,)), ((), ())), preferred_element_type=f32
    )
    ge[r0 : r0 + R, :] = ge[r0 : r0 + R, :] + ((o[:R, :emb] + o[:R, emb:]) + o[R:, :emb])


def unit(u, R, emb, width, pc, rhs, rd, ll, ld, scs, acc, ge, en):
    todo = [(k, n) for n in range(0, 2 * width, 256) for k in range(3)]
    chunks = list(range(0, 2 * width, R))
    strips = list(range(0, R, 16))
    per = -(-len(todo) // len(strips))
    for k, n in todo:
        dot_piece(k, n, u, chunks[0], R, rhs, rd, ll, ld, scs[0])
    for i, r0 in enumerate(chunks):
        later = list(todo) if i + 1 < len(chunks) else []
        for j, s in enumerate(strips):
            strip(s, u, r0, R, width, pc, acc, en, scs[i % NBUF])
            if j == 0 and i > 0:
                grad_dot(u, chunks[i - 1], R, emb, rhs, ge, scs[(i - 1) % NBUF])
            for _ in range(per):
                if later:
                    k, n = later.pop(0)
                    dot_piece(k, n, u, chunks[i + 1], R, rhs, rd, ll, ld, scs[(i + 1) % NBUF])
    grad_dot(u, chunks[-1], R, emb, rhs, ge, scs[(len(chunks) - 1) % NBUF])


def finish(weight, emb, width, acc, ge, tp, gres, pres):
    for s in range(2):
        rs = slice(s * width, (s + 1) * width)
        gres[s] = jnp.transpose(ge[rs, :]) * (weight / (4.0 * math.sqrt(emb)))
        cols = lax.broadcasted_iota(jnp.int32, (width, LANE), 1)
        for f in range(2):
            ss = jnp.sum(acc[4 * f, rs, :], axis=1, keepdims=True)
            tt = jnp.zeros((width, LANE), f32)
            for c in range(3):
                tc = jnp.sum(acc[4 * f + 1 + c, rs, :], axis=1, keepdims=True)
                tt = tt + jnp.where(cols == c, tc, 0.0)
            res = (ss * tp[f, rs, :] - tt) * (weight if f else -weight)
            pres[s, f] = jnp.transpose(res)[0:8, :]


def kernel(
    R, emb, width, tracks, frames,
    e_ref, pm_ref, gemb, gpos, lout,
    buf, pc, mid, rhs, rd, ll, ld, tp, acc, ge, en, gres, pres, prec, l1, l2,
    *rest,
):
    scs = [rest[4 * i : 4 * i + 4] for i in range(NBUF)]
    r1, s1, rg, sg, rr, sr, rl, sl = rest[4 * NBUF :]
    weight = rigidity / math.sqrt(tracks)
    n_track, n_tm = 16, 16
    track, tm = lax.axis_index("track"), lax.axis_index("tm")
    z, xl = track // 2, lax.rem(track, 2)
    plane, core = tm // 2, lax.rem(tm, 2)
    step = z // 2

    cur_to, next_to = [], []
    for l in range(2):
        f = 2 * core + l
        dz, slot, other = owner(z, f)
        cur_to.append((2 * dz + xl, 2 * plane + flip(core, other), slot))
        s = lax.rem(f + STEPS - 1, STEPS)
        back = jnp.where(f == 0, 1, 0)
        dz, slot, other = owner(z, s)
        next_to.append((2 * dz + xl, 2 * lax.rem(plane + PLANES - back, PLANES) + flip(s // 2, other), slot))
    home = step // 2
    mine = flip(core, home)
    sign = 2 * lax.rem(z, 2) - 1
    last = jnp.where(step == STEPS - 1, 1, 0)
    n_frame = lax.rem(step + 1, STEPS)
    n_tmid = 2 * lax.rem(plane + last, PLANES) + n_frame // 2
    cur_of, next_of = [], []
    for s in range(2):
        away = mine if s == 0 else 3 - mine
        zt = 2 * lax.rem(z + sign * away + ROWS, ROWS) + xl
        cur_of.append((zt, 2 * plane + home))
        next_of.append((zt, n_tmid))

    barrier = pltpu.get_barrier_semaphore()

    def greet(t, m):
        other = (t != track) | (m != tm)

        @pl.when(other)
        def _():
            pl.semaphore_signal(barrier, inc=1, device_id=(t, m), device_id_type=MESH)

        return jnp.where(other, 1, 0)

    met = n_track - 1 + n_tm - 1
    for t, m, _ in cur_to + next_to:
        met = met + greet(t, m)
    for t, m in cur_of + next_of:
        met = met + greet(t, m)
    for k in range(1, n_track):
        pl.semaphore_signal(barrier, inc=1, device_id=(lax.rem(track + k, n_track), tm), device_id_type=MESH)
    for k in range(1, n_tm):
        pl.semaphore_signal(barrier, inc=1, device_id=(track, lax.rem(tm + k, n_tm)), device_id_type=MESH)

    acc[...] = jnp.zeros_like(acc)
    ge[...] = jnp.zeros_like(ge)
    en[...] = jnp.zeros_like(en)
    pl.semaphore_wait(barrier, met)

    def send(src, dst, ssem, rsem, t, m, start=True):
        same = (t == track) & (m == tm)
        if start:

            @pl.when(same)
            def _():
                pltpu.make_async_copy(src, dst, rsem).start()

        @pl.when(jnp.logical_not(same))
        def _():
            there = pltpu.make_async_remote_copy(
                src_ref=src, dst_ref=dst, send_sem=ssem, recv_sem=rsem, device_id=(t, m), device_id_type=MESH
            )
            there.start() if start else there.wait_send()

    def arrive(ref, sem):
        pltpu.make_async_copy(ref, ref, sem).wait()

    def stage1(start):
        for l in range(2):
            t, m, slot = cur_to[l]
            tn, mn, slot_n = next_to[l]
            send(pm_ref.at[l], buf.at[0, slot, pl.ds(emb, 8)], s1.at[0, l], r1.at[0, slot], t, m, start)
            send(pm_ref.at[l], buf.at[0, slot_n, pl.ds(emb + 8, 8)], s1.at[1, l], r1.at[1, slot_n], tn, mn, start)
            send(e_ref.at[l], buf.at[0, slot, pl.ds(0, emb)], s1.at[2, l], r1.at[2, slot], t, m, start)

    peers = {
        1: (track, flip(core, 1) + 2 * plane),
        2: (2 * z + 1 - xl, tm),
        4: (2 * (z - sign * 1) + xl, tm),
    }

    def pass_on(n, src, dst, slot, via):
        t, m = peers[via]
        return pltpu.make_async_remote_copy(
            src_ref=buf.at[src, slot], dst_ref=buf.at[dst, slot], send_sem=sg.at[n], recv_sem=rg.at[dst, slot],
            device_id=(t, m), device_id_type=MESH,
        )

    first = [[pass_on(3 * s + k, 0, v, s, v) for k, v in enumerate((2, 4, 1))] for s in range(2)]
    second = [pass_on(6 + s, 2, 3, s, 1) for s in range(2)] + [pass_on(8 + s, 4, 5, s, 1) for s in range(2)]
    across = [pass_on(10, 2, 6, 0, 4), pass_on(11, 4, 6, 1, 2)]
    third = [pass_on(12 + s, 6, 7, s, 1) for s in range(2)]

    stage1(True)
    for s in range(2):
        arrive(buf.at[0, s, pl.ds(emb, 8)], r1.at[0, s])
        arrive(buf.at[0, s, pl.ds(emb + 8, 8)], r1.at[1, s])
        arrive(buf.at[0, s, pl.ds(0, emb)], r1.at[2, s])
        for c in first[s]:
            c.start()
    valid = jnp.where((plane == PLANES - 1) & (step == STEPS - 1), 0.0, 1.0)
    prep_rows(valid, emb, width, buf, mid, ll, ld, tp)

    def landed(u):
        for s in range(2):
            arrive(buf.at[u, s], rg.at[u, s])

    @pl.loop(0, 8)
    def _(i):
        u = i + jnp.where(i == 3, 1, 0) - jnp.where(i == 4, 1, 0)

        @pl.when(i == 1)
        def _():
            landed(1)

        @pl.when(i == 2)
        def _():
            landed(2)
            across[0].start()
            second[0].start()
            second[1].start()
            landed(4)
            across[1].start()
            second[2].start()
            second[3].start()

        @pl.when(i == 4)
        def _():
            landed(6)
            third[0].start()
            third[1].start()
            landed(3)

        @pl.when(i == 5)
        def _():
            landed(5)

        @pl.when(i == 7)
        def _():
            landed(7)

        prep_cols(u, emb, width, buf, pc, mid, rhs, rd)
        unit(u, R, emb, width, pc, rhs, rd, ll, ld, scs, acc, ge, en)

    def round_of(n, group, here, size, send_at):
        return [
            pltpu.make_async_remote_copy(
                src_ref=group.at[here], dst_ref=group.at[here], send_sem=sl.at[n, k - 1], recv_sem=rl.at[n, here],
                device_id=send_at(lax.rem(here + k, size)), device_id_type=MESH,
            )
            for k in range(1, size)
        ]

    def gathered(n, group, here, size):
        for k in range(1, size):
            at = lax.rem(here + k, size)
            arrive(group.at[at], rl.at[n, at])

    l1[track] = en[...]
    round1 = round_of(0, l1, track, n_track, lambda t: (t, tm))
    for c in round1:
        c.start()

    finish(weight, emb, width, acc, ge, tp, gres, pres)

    def stage3(start):
        for s in range(2):
            t, m = cur_of[s]
            tn, mn = next_of[s]
            l = lax.rem(step, 2)
            ln = lax.rem(n_frame, 2)
            send(pres.at[s, 0], prec.at[l, 0], sr.at[0, s], rr.at[0, l], t, m, start)
            send(pres.at[s, 1], prec.at[ln, 1], sr.at[1, s], rr.at[1, ln], tn, mn, start)
            send(gres.at[s], gemb.at[l], sr.at[2, s], rr.at[2, l], t, m, start)

    stage3(True)
    gathered(0, l1, track, n_track)
    l2[tm] = jnp.sum(l1[...], axis=0)
    round2 = round_of(1, l2, tm, n_tm, lambda m: (track, m))
    for c in round2:
        c.start()
    for l in range(2):
        arrive(prec.at[l, 0], rr.at[0, l])
        arrive(prec.at[l, 1], rr.at[1, l])
        gpos[l] = prec[l, 0] + prec[l, 1]
        arrive(gemb.at[l], rr.at[2, l])
    gathered(1, l2, tm, n_tm)
    pairs = tracks * (tracks - 1) / 2.0 * (frames - 1)
    total = jnp.sum(jnp.sum(jnp.sum(l2[...], axis=0), axis=0, keepdims=True), axis=1, keepdims=True)
    lout[...] = jnp.broadcast_to(total * (0.25 / pairs), lout.shape)

    stage1(False)
    for c in first[0] + first[1] + second + across + third + round1 + round2:
        c.wait_send()
    stage3(False)


def on_device(positions, embeddings, visible):
    frames_local, emb, width = embeddings.shape
    tracks = width * lax.axis_size("track")
    frames = frames_local * lax.axis_size("tm")
    seen = visible.astype(f32)
    pm = jnp.concatenate(
        [jnp.swapaxes(positions, 0, 1), seen[:, None], jnp.zeros((frames_local, 4, width), f32)], 1
    )
    R = width // 2
    C = 2 * width
    K = 3 * emb + LANE
    dma, vmem = pltpu.SemaphoreType.DMA, pltpu.VMEM
    scratch = [
        vmem((8, 2, emb + 16, width), f32),
        vmem((8, 2, 16, width), f32),
        vmem((16, LANE), f32),
        vmem((8, K, C), bf16),
        vmem((8, 2, 32, C), bf16),
        vmem((C, K), bf16),
        vmem((2, C, 32), bf16),
        vmem((2, C, LANE), f32),
        vmem((8, C, LANE), f32),
        vmem((C, emb), f32),
        vmem((8, LANE), f32),
        vmem((2, emb, width), f32),
        vmem((2, 2, 8, width), f32),
        vmem((2, 2, 8, width), f32),
        vmem((16, 8, LANE), f32),
        vmem((16, 8, LANE), f32),
    ]
    for _ in range(NBUF):
        scratch += [vmem((R, C), f32)] * 3 + [vmem((2 * R, C), bf16)]
    scratch += [dma((3, 2)), dma((3, 2)), dma((8, 2)), dma((14,)), dma((3, 2)), dma((3, 2)), dma((2, 16)), dma((2, 15))]
    whole = pl.BlockSpec(memory_space=pltpu.VMEM)
    grad_emb, grad_pos, loss = pl.pallas_call(
        functools.partial(kernel, R, emb, width, tracks, frames),
        out_shape=[
            jax.ShapeDtypeStruct((2, emb, width), f32),
            jax.ShapeDtypeStruct((2, 8, width), f32),
            jax.ShapeDtypeStruct((8, LANE), f32),
        ],
        in_specs=[whole, whole],
        out_specs=[whole] * 3,
        scratch_shapes=scratch,
        compiler_params=pltpu.CompilerParams(
            collective_id=0, has_side_effects=True, vmem_limit_bytes=60 * 2**20
        ),
    )(embeddings, pm)
    return (jnp.swapaxes(grad_pos[:, :3], 0, 1), grad_emb, loss[0, 0])


def solution(mesh):
    in_specs = (P(None, "tm", "track"), P("tm", None, "track"), P("tm", "track"))
    out_specs = (P(None, "tm", "track"), P("tm", None, "track"), P())
    return jax.shard_map(
        on_device, mesh=mesh, in_specs=in_specs, out_specs=out_specs, check_vma=False
    )
```

```python
import functools
import math

import jax
import jax.numpy as jnp
from jax import lax
from jax.experimental import pallas as pl
from jax.experimental.pallas import tpu as pltpu
from jax.sharding import PartitionSpec as P

f32, bf16 = jnp.float32, jnp.bfloat16
MESH = pl.DeviceIdType.MESH
rigidity = 4.0
HIDE = 2.0**20
LANE = 128
ENERGY = True
NBUF = 2

ROWS = 8
PLANES = 8
STEPS = 4


def owner(z, f):
    rel = lax.rem(z - 2 * f + 2 * ROWS, ROWS)
    upper = jnp.where((rel >= 1) & (rel <= 4), 1, 0)
    away = jnp.where(upper == 1, rel - 1, lax.rem(ROWS - rel, ROWS))
    other = jnp.where((away == 1) | (away == 2), 1, 0)
    slot = jnp.where(away >= 2, 1, 0)
    return 2 * f + upper, slot, other


def flip(core, other):
    return core + other - 2 * core * other


def split2(v):
    hi = v.astype(bf16)
    return hi, (v - hi.astype(f32)).astype(bf16)


def pieces(v):
    h = v.astype(bf16).astype(f32)
    m = (v - h).astype(bf16).astype(f32)
    return h, m, (v - h - m).astype(bf16).astype(f32)


def prep_cols(chip, s, emb, width, buf, pc, mid, rhs, rd):
    g = 2 * chip + s
    for half in range(2):
        u = 2 * chip + half
        cs = slice(half * width, (half + 1) * width)
        hi, lo = split2(buf[u, s, 0:emb, :])
        rhs[g, 0:emb, cs] = hi
        rhs[g, emb : 2 * emb, cs] = lo
        rhs[g, 2 * emb : 3 * emb, cs] = hi
        q = buf[u, s, emb + 3 : emb + 4, :] * buf[u, s, emb + 11 : emb + 12, :]
        rows = lax.broadcasted_iota(jnp.int32, (LANE, width), 0)
        m = jnp.where(rows == 0, 1.0, 0.0) + jnp.where(rows == 1, (q - 1.0) * HIDE, 0.0)
        rhs[g, 3 * emb :, cs] = m.astype(bf16)
        for f in range(2):
            p = [
                buf[u, s, emb + 8 * f + c : emb + 8 * f + c + 1, :] - mid[8 * f + c : 8 * f + c + 1, 0:1]
                for c in range(3)
            ]
            out = []
            for c in range(3):
                pc[g, half, 8 * f + c : 8 * f + c + 1, :] = p[c]
                h, mm, l = pieces(p[c])
                out += [h, mm, h, mm, l, h]
            n = p[0] * p[0] + p[1] * p[1] + p[2] * p[2]
            one = jnp.ones_like(n)
            out += [one, one, one] + list(pieces(n)) + [jnp.zeros((8, width), f32)]
            rd[g, f, :, cs] = jnp.concatenate(out, 0).astype(bf16)


def prep_rows(sides, valid, emb, width, buf, mid, ll, ld, tp):
    if 0 in sides:
        mean = jnp.sum(buf[0, 0, emb:, :], 1, keepdims=True) / width
        mid[...] = jnp.broadcast_to(mean, mid.shape)
    for s in sides:
        rs = slice(s * width, (s + 1) * width)
        hi, lo = split2(jnp.transpose(buf[0, s, 0:emb, :]) * (0.5 / math.sqrt(emb)))
        ll[rs, 0:emb] = hi
        ll[rs, emb : 2 * emb] = hi
        ll[rs, 2 * emb : 3 * emb] = lo
        q = buf[0, s, emb + 3 : emb + 4, :] * buf[0, s, emb + 11 : emb + 12, :] * valid
        one = jnp.ones_like(q)
        m = jnp.concatenate([(q - 1.0) * HIDE, one, jnp.zeros((LANE - 2, width), f32)], 0)
        ll[rs, 3 * emb :] = jnp.transpose(m).astype(bf16)
        for f in range(2):
            p = [
                buf[0, s, emb + 8 * f + c : emb + 8 * f + c + 1, :] - mid[8 * f + c : 8 * f + c + 1, 0:1]
                for c in range(3)
            ]
            out = []
            for c in range(3):
                h, mm, l = pieces(p[c])
                out += [-2.0 * h, -2.0 * h, -2.0 * mm, -2.0 * mm, -2.0 * h, -2.0 * l]
            n = p[0] * p[0] + p[1] * p[1] + p[2] * p[2] + 1.0
            out += list(pieces(n)) + [one, one, one, jnp.zeros((LANE - 24, width), f32)]
            ld[f, rs, :] = jnp.transpose(jnp.concatenate(out, 0)).astype(bf16)[:, 0:32]
            tp[f, rs, :] = jnp.transpose(jnp.concatenate(p + [jnp.zeros((LANE - 3, width), f32)], 0))


def dot_piece(k, n0, n1, u, r0, R, rhs, rd, ll, ld, sc):
    ns = slice(n0, n1)
    rows = slice(r0, r0 + R)
    if k == 0:
        sc[0][:, ns] = jnp.dot(ll[rows, :], rhs[u, :, ns], preferred_element_type=f32)
    else:
        sc[k][:, ns] = jnp.dot(ld[k - 1, rows, :], rd[u, k - 1, :, ns], preferred_element_type=f32)


def strip(s, u, r0, cols, width, pc, acc, en, energy, sc):
    xs, d0s, d1s, gs = sc
    R = xs.shape[0]
    at = slice(r0 + s, r0 + s + 16)
    A = [acc[k, at, :] for k in range(8)]
    es = en[...] if energy else None
    for c0 in range(cols[0], cols[1], 256):
        c1 = min(c0 + 256, cols[1])
        cs = slice(c0, c1)
        x, a0, a1 = xs[s : s + 16, cs], d0s[s : s + 16, cs], d1s[s : s + 16, cs]
        q0, q1 = lax.rsqrt(a0), lax.rsqrt(a1)
        ch = a1 * q1 - a0 * q0
        v = jnp.tanh(x) * ch
        h = ch + v
        g = h * (ch - v)
        hi = g.astype(bf16)
        gs[s : s + 16, cs] = hi
        gs[R + s : R + s + 16, cs] = (g - hi.astype(f32)).astype(bf16)
        e = h * ch if energy else None
        w = (h * q0, h * q1)
        for k in range(0, c1 - c0, LANE):
            j = c0 + k
            side, js = j // width, slice(j % width, j % width + LANE)
            for f in range(2):
                wk = w[f][:, k : k + LANE]
                A[4 * f] = A[4 * f] + wk
                for c in range(3):
                    A[4 * f + 1 + c] = A[4 * f + 1 + c] + wk * pc[u, side, 8 * f + c : 8 * f + c + 1, js]
            if energy:
                es = es + (e[0:8, k : k + LANE] + e[8:16, k : k + LANE])
    for k in range(8):
        acc[k, at, :] = A[k]
    if energy:
        en[...] = es


def grad_dot(u, r0, cols, emb, rhs, ge, sc):
    R = sc[0].shape[0]
    cs = slice(*cols)
    o = lax.dot_general(
        sc[3][:, cs], rhs[u, 0 : 2 * emb, cs], (((1,), (1,)), ((), ())), preferred_element_type=f32
    )
    rows = slice(r0, r0 + R)
    ge[rows, :] = ge[rows, :] + ((o[:R, :emb] + o[:R, emb:]) + o[R:, :emb])


def tiles(jobs, energy, emb, width, pc, rhs, rd, ll, ld, scs, acc, ge, en):
    R = scs[0][0].shape[0]
    cols = (0, 2 * width)
    parts = [(k, n, n + 256) for n in range(0, 2 * width, 256) for k in range(3)]
    strips = list(range(0, R, 16))
    for part in parts:
        dot_piece(*part, jobs[0][1], jobs[0][0], R, rhs, rd, ll, ld, scs[0])
    for i, (r0, u) in enumerate(jobs):
        later = list(parts) if i + 1 < len(jobs) else []
        per = -(-len(later) // len(strips))
        for j, s in enumerate(strips):
            strip(s, u, r0, cols, width, pc, acc, en, energy, scs[i % NBUF])
            if j == 0 and i > 0:
                grad_dot(jobs[i - 1][1], jobs[i - 1][0], cols, emb, rhs, ge, scs[(i - 1) % NBUF])
            for _ in range(per):
                if later:
                    dot_piece(*later.pop(0), jobs[i + 1][1], jobs[i + 1][0], R, rhs, rd, ll, ld, scs[(i + 1) % NBUF])
    grad_dot(jobs[-1][1], jobs[-1][0], cols, emb, rhs, ge, scs[(len(jobs) - 1) % NBUF])


def finish(sides, weight, emb, width, acc, ge, tp, gres, pres):
    for s in sides:
        rs = slice(s * width, (s + 1) * width)
        gres[s] = jnp.transpose(ge[rs, :]) * (weight / (4.0 * math.sqrt(emb)))
        cols = lax.broadcasted_iota(jnp.int32, (width, LANE), 1)
        for f in range(2):
            ss = jnp.sum(acc[4 * f, rs, :], axis=1, keepdims=True)
            tt = jnp.zeros((width, LANE), f32)
            for c in range(3):
                tc = jnp.sum(acc[4 * f + 1 + c, rs, :], axis=1, keepdims=True)
                tt = tt + jnp.where(cols == c, tc, 0.0)
            res = (ss * tp[f, rs, :] - tt) * (weight if f else -weight)
            pres[s, f] = jnp.transpose(res)[0:8, :]


def kernel(
    R, emb, width, tracks, frames,
    pos, emb_in, vis, gpos, gemb, lout,
    pos_v, vis_v, e_ref, pm_ref, sin, buf, pc, mid, rhs, rd, ll, ld, tp, acc, ge, en, ent, gres, pres, prec, l1, l2,
    *rest,
):
    scs = [rest[4 * i : 4 * i + 4] for i in range(NBUF)]
    r1, s1, rg, sg, rr, sr, rl, sl = rest[4 * NBUF :]
    weight = rigidity / math.sqrt(tracks)
    n_track, n_tm = 16, 16
    track, tm = lax.axis_index("track"), lax.axis_index("tm")
    z, xl = track // 2, lax.rem(track, 2)
    plane, core = tm // 2, lax.rem(tm, 2)
    step = z // 2

    cur_to, next_to = [], []
    for l in range(2):
        f = 2 * core + l
        dz, slot, other = owner(z, f)
        cur_to.append((2 * dz + xl, 2 * plane + flip(core, other), slot))
        s = lax.rem(f + STEPS - 1, STEPS)
        back = jnp.where(f == 0, 1, 0)
        dz, slot, other = owner(z, s)
        next_to.append((2 * dz + xl, 2 * lax.rem(plane + PLANES - back, PLANES) + flip(s // 2, other), slot))
    home = step // 2
    mine = flip(core, home)
    sign = 2 * lax.rem(z, 2) - 1
    last = jnp.where(step == STEPS - 1, 1, 0)
    n_frame = lax.rem(step + 1, STEPS)
    n_tmid = 2 * lax.rem(plane + last, PLANES) + n_frame // 2
    cur_of, next_of = [], []
    for s in range(2):
        away = mine if s == 0 else 3 - mine
        zt = 2 * lax.rem(z + sign * away + ROWS, ROWS) + xl
        cur_of.append((zt, 2 * plane + home))
        next_of.append((zt, n_tmid))

    barrier = pltpu.get_barrier_semaphore()

    def greet(t, m):
        other = (t != track) | (m != tm)

        @pl.when(other)
        def _():
            pl.semaphore_signal(barrier, inc=1, device_id=(t, m), device_id_type=MESH)

        return jnp.where(other, 1, 0)

    met = n_track - 1 + n_tm - 1
    for t, m, _ in cur_to + next_to:
        met = met + greet(t, m)
    for t, m in cur_of + next_of:
        met = met + greet(t, m)
    for k in range(1, n_track):
        pl.semaphore_signal(barrier, inc=1, device_id=(lax.rem(track + k, n_track), tm), device_id_type=MESH)
    for k in range(1, n_tm):
        pl.semaphore_signal(barrier, inc=1, device_id=(track, lax.rem(tm + k, n_tm)), device_id_type=MESH)

    bring = [
        pltpu.make_async_copy(pos, pos_v, sin.at[0]),
        pltpu.make_async_copy(vis, vis_v, sin.at[1]),
        pltpu.make_async_copy(emb_in, e_ref, sin.at[2]),
    ]
    for c in bring:
        c.start()
    acc[...] = jnp.zeros_like(acc)
    ge[...] = jnp.zeros_like(ge)
    en[...] = jnp.zeros_like(en)
    ent[...] = jnp.zeros_like(ent)
    for c in bring:
        c.wait()
    for l in range(2):
        rows = [pos_v[c, l : l + 1, :] for c in range(3)] + [vis_v[l : l + 1, :].astype(f32)]
        pm_ref[l] = jnp.concatenate(rows + [jnp.zeros((4, width), f32)], 0)
    pl.semaphore_wait(barrier, met)

    def send(src, dst, ssem, rsem, t, m, start=True):
        same = (t == track) & (m == tm)
        if start:

            @pl.when(same)
            def _():
                pltpu.make_async_copy(src, dst, rsem).start()

        @pl.when(jnp.logical_not(same))
        def _():
            there = pltpu.make_async_remote_copy(
                src_ref=src, dst_ref=dst, send_sem=ssem, recv_sem=rsem, device_id=(t, m), device_id_type=MESH
            )
            there.start() if start else there.wait_send()

    def arrive(ref, sem):
        pltpu.make_async_copy(ref, ref, sem).wait()

    def stage1(start):
        for l in range(2):
            t, m, slot = cur_to[l]
            tn, mn, slot_n = next_to[l]
            send(pm_ref.at[l], buf.at[0, slot, pl.ds(emb, 8)], s1.at[0, l], r1.at[0, slot], t, m, start)
            send(pm_ref.at[l], buf.at[0, slot_n, pl.ds(emb + 8, 8)], s1.at[1, l], r1.at[1, slot_n], tn, mn, start)

    def stage1_emb(slots, start):
        for l in range(2):
            t, m, slot = cur_to[l]

            def go():
                send(e_ref.at[l], buf.at[0, slot, pl.ds(0, emb)], s1.at[2, l], r1.at[2, slot], t, m, start)

            if slots is None:
                go()
            else:
                pl.when(slot == slots)(go)

    peers = {
        1: (track, flip(core, 1) + 2 * plane),
        2: (2 * z + 1 - xl, tm),
        4: (2 * (z - sign * 1) + xl, tm),
    }

    def pass_on(n, src, dst, slot, via):
        t, m = peers[via]
        return pltpu.make_async_remote_copy(
            src_ref=buf.at[src, slot], dst_ref=buf.at[dst, slot], send_sem=sg.at[n], recv_sem=rg.at[dst, slot],
            device_id=(t, m), device_id_type=MESH,
        )

    first = [[pass_on(3 * s + k, 0, v, s, v) for k, v in enumerate((2, 4, 1))] for s in range(2)]
    second = [pass_on(6 + s, 2, 3, s, 1) for s in range(2)] + [pass_on(8 + s, 4, 5, s, 1) for s in range(2)]
    across = [pass_on(10, 2, 6, 0, 4), pass_on(11, 4, 6, 1, 2)]
    third = [pass_on(12 + s, 6, 7, s, 1) for s in range(2)]

    stage1_emb(0, True)
    stage1(True)
    valid = jnp.where((plane == PLANES - 1) & (step == STEPS - 1), 0.0, 1.0)

    def own(s):
        arrive(buf.at[0, s, pl.ds(emb, 8)], r1.at[0, s])
        arrive(buf.at[0, s, pl.ds(emb + 8, 8)], r1.at[1, s])
        arrive(buf.at[0, s, pl.ds(0, emb)], r1.at[2, s])
        for c in first[s]:
            c.start()
        prep_rows((s,), valid, emb, width, buf, mid, ll, ld, tp)

    def landed(u, s):
        arrive(buf.at[u, s], rg.at[u, s])

    own(0)

    def stage3(s, start):
        t, m = cur_of[s]
        tn, mn = next_of[s]
        l = lax.rem(step, 2)
        ln = lax.rem(n_frame, 2)
        send(gres.at[s], gemb.at[l], sr.at[2, s], rr.at[2, l], t, m, start)
        send(pres.at[s, 0], prec.at[l, 0], sr.at[0, s], rr.at[0, l], t, m, start)
        send(pres.at[s, 1], prec.at[ln, 1], sr.at[1, s], rr.at[1, ln], tn, mn, start)

    def round_of(n, group, here, size, send_at):
        return [
            pltpu.make_async_remote_copy(
                src_ref=group.at[here], dst_ref=group.at[here], send_sem=sl.at[n, k - 1], recv_sem=rl.at[n, here],
                device_id=send_at(lax.rem(here + k, size)), device_id_type=MESH,
            )
            for k in range(1, size)
        ]

    def gathered(n, group, here, size):
        for k in range(1, size):
            at = lax.rem(here + k, size)
            arrive(group.at[at], rl.at[n, at])

    cols = (emb, width, buf, pc, mid, rhs, rd)
    work = (emb, width, pc, rhs, rd, ll, ld, scs, acc, ge, en)

    @pl.loop(0, 4)
    def _(chip):
        @pl.when(chip == 0)
        def _():
            landed(1, 0)
            stage1_emb(1, True)

        @pl.when(chip == 1)
        def _():
            landed(2, 0)
            across[0].start()
            second[0].start()
            landed(4, 0)
            second[2].start()
            landed(3, 0)

        @pl.when(chip == 2)
        def _():
            landed(5, 0)

        @pl.when(chip == 3)
        def _():
            landed(6, 0)
            third[0].start()
            own(1)
            landed(7, 0)

        prep_cols(chip, 0, *cols)
        tiles([(0, 2 * chip)], True, *work)

    ent[...] = en[...]
    en[...] = jnp.zeros_like(en)

    @pl.loop(0, 4)
    def _(i):
        @pl.when(i == 1)
        def _():
            landed(2, 1)
            second[1].start()
            landed(4, 1)
            across[1].start()
            second[3].start()

        @pl.when(i == 2)
        def _():
            landed(1, 1)
            landed(3, 1)
            prep_cols(0, 1, *cols)
            prep_cols(1, 1, *cols)
            ent[...] = ent[...] + 2.0 * en[...]
            en[...] = jnp.zeros_like(en)

        @pl.when(i == 3)
        def _():
            landed(6, 1)
            third[1].start()
            landed(5, 1)
            prep_cols(2, 1, *cols)
            landed(7, 1)
            prep_cols(3, 1, *cols)

        g = 4 * lax.rem(i, 2) + i // 2
        tiles([(width, g), (width, g + 2)], True, *work)

    l1[track] = ent[...] + en[...]
    finish((1,), weight, emb, width, acc, ge, tp, gres, pres)
    round1 = round_of(0, l1, track, n_track, lambda t: (t, tm))
    round2 = round_of(1, l2, tm, n_tm, lambda m: (track, m))
    for c in round1:
        c.start()
    stage3(1, True)

    @pl.loop(0, 2)
    def _(i):
        @pl.when(i == 1)
        def _():
            gathered(0, l1, track, n_track)
            l2[tm] = jnp.sum(l1[...], axis=0)
            for c in round2:
                c.start()

        tiles([(0, 4 * i + 1), (0, 4 * i + 3)], ENERGY, *work)

    finish((0,), weight, emb, width, acc, ge, tp, gres, pres)
    stage3(0, True)
    for l in range(2):
        arrive(prec.at[l, 0], rr.at[0, l])
        arrive(prec.at[l, 1], rr.at[1, l])
        for c in range(3):
            gpos[c, l : l + 1, :] = prec[l, 0, c : c + 1, :] + prec[l, 1, c : c + 1, :]
        arrive(gemb.at[l], rr.at[2, l])
    gathered(1, l2, tm, n_tm)
    pairs = tracks * (tracks - 1) / 2.0 * (frames - 1)
    total = jnp.sum(jnp.sum(jnp.sum(l2[...], axis=0), axis=0, keepdims=True), axis=1, keepdims=True)
    lout[...] = total * (0.25 / pairs)

    stage1(False)
    stage1_emb(None, False)
    for c in first[0] + first[1] + second + across + third + round1 + round2:
        c.wait_send()
    for s in range(2):
        stage3(s, False)


def on_device(positions, embeddings, visible):
    frames_local, emb, width = embeddings.shape
    tracks = width * lax.axis_size("track")
    frames = frames_local * lax.axis_size("tm")
    R = width
    C = 2 * width
    K = 3 * emb + LANE
    dma, vmem = pltpu.SemaphoreType.DMA, pltpu.VMEM
    scratch = [
        vmem((3, 2, width), f32),
        vmem((2, width), jnp.int32),
        vmem((2, emb, width), f32),
        vmem((2, 8, width), f32),
        dma((3,)),
        vmem((8, 2, emb + 16, width), f32),
        vmem((8, 2, 16, width), f32),
        vmem((16, LANE), f32),
        vmem((8, K, C), bf16),
        vmem((8, 2, 32, C), bf16),
        vmem((C, K), bf16),
        vmem((2, C, 32), bf16),
        vmem((2, C, LANE), f32),
        vmem((8, C, LANE), f32),
        vmem((C, emb), f32),
        vmem((8, LANE), f32),
        vmem((8, LANE), f32),
        vmem((2, emb, width), f32),
        vmem((2, 2, 8, width), f32),
        vmem((2, 2, 8, width), f32),
        vmem((16, 8, LANE), f32),
        vmem((16, 8, LANE), f32),
    ]
    for _ in range(NBUF):
        scratch += [vmem((R, C), f32)] * 3 + [vmem((2 * R, C), bf16)]
    scratch += [dma((3, 2)), dma((3, 2)), dma((8, 2)), dma((14,)), dma((3, 2)), dma((3, 2)), dma((2, 16)), dma((2, 15))]
    whole, there = pl.BlockSpec(memory_space=pltpu.VMEM), pl.BlockSpec(memory_space=pl.ANY)
    grad_pos, grad_emb, loss = pl.pallas_call(
        functools.partial(kernel, R, emb, width, tracks, frames),
        out_shape=[
            jax.ShapeDtypeStruct((3, 2, width), f32),
            jax.ShapeDtypeStruct((2, emb, width), f32),
            jax.ShapeDtypeStruct((1, 1), f32),
        ],
        in_specs=[there] * 3,
        out_specs=[whole] * 3,
        scratch_shapes=scratch,
        compiler_params=pltpu.CompilerParams(
            collective_id=0, has_side_effects=True, vmem_limit_bytes=60 * 2**20
        ),
    )(positions, embeddings, visible)
    return (grad_pos, grad_emb, loss.reshape(()))


def solution(mesh):
    in_specs = (P(None, "tm", "track"), P("tm", None, "track"), P("tm", "track"))
    out_specs = (P(None, "tm", "track"), P("tm", None, "track"), P())
    return jax.shard_map(
        on_device, mesh=mesh, in_specs=in_specs, out_specs=out_specs, check_vma=False
    )
```

```python
import functools
import math

import jax
import jax.numpy as jnp
from jax import lax
from jax.experimental import pallas as pl
from jax.experimental.pallas import tpu as pltpu
from jax.sharding import PartitionSpec as P

f32, bf16 = jnp.float32, jnp.bfloat16
MESH = pl.DeviceIdType.MESH
rigidity = 4.0
HIDE = 2.0**20
LANE = 128
ENERGY = True
NBUF = 2

ROWS = 8
PLANES = 8
STEPS = 4


def owner(z, f):
    rel = lax.rem(z - 2 * f + 2 * ROWS, ROWS)
    upper = jnp.where((rel >= 1) & (rel <= 4), 1, 0)
    away = jnp.where(upper == 1, rel - 1, lax.rem(ROWS - rel, ROWS))
    other = jnp.where((away == 1) | (away == 2), 1, 0)
    slot = jnp.where(away >= 2, 1, 0)
    return 2 * f + upper, slot, other


def flip(core, other):
    return core + other - 2 * core * other


def split2(v):
    hi = v.astype(bf16)
    return hi, (v - hi.astype(f32)).astype(bf16)


def pieces(v):
    h = v.astype(bf16).astype(f32)
    m = (v - h).astype(bf16).astype(f32)
    return h, m, (v - h - m).astype(bf16).astype(f32)


def prep_cols(chip, s, emb, width, buf, pc, mid, rhs, rd):
    g = 2 * chip + s
    for half in range(2):
        u = 2 * chip + half
        cs = slice(half * width, (half + 1) * width)
        hi, lo = split2(buf[u, s, 0:emb, :])
        rhs[g, 0:emb, cs] = hi
        rhs[g, emb : 2 * emb, cs] = lo
        rhs[g, 2 * emb : 3 * emb, cs] = hi
        q = buf[u, s, emb + 3 : emb + 4, :] * buf[u, s, emb + 11 : emb + 12, :]
        rows = lax.broadcasted_iota(jnp.int32, (LANE, width), 0)
        m = jnp.where(rows == 0, 1.0, 0.0) + jnp.where(rows == 1, (q - 1.0) * HIDE, 0.0)
        rhs[g, 3 * emb :, cs] = m.astype(bf16)
        for f in range(2):
            p = [
                buf[u, s, emb + 8 * f + c : emb + 8 * f + c + 1, :] - mid[8 * f + c : 8 * f + c + 1, 0:1]
                for c in range(3)
            ]
            out = []
            for c in range(3):
                pc[g, half, 8 * f + c : 8 * f + c + 1, :] = p[c]
                h, mm, l = pieces(p[c])
                out += [h, mm, h, mm, l, h]
            n = p[0] * p[0] + p[1] * p[1] + p[2] * p[2]
            one = jnp.ones_like(n)
            out += [one, one, one] + list(pieces(n)) + [jnp.zeros((8, width), f32)]
            rd[g, f, :, cs] = jnp.concatenate(out, 0).astype(bf16)


def prep_rows(sides, valid, emb, width, buf, mid, ll, ld, tp):
    if 0 in sides:
        mean = jnp.sum(buf[0, 0, emb:, :], 1, keepdims=True) / width
        mid[...] = jnp.broadcast_to(mean, mid.shape)
    for s in sides:
        rs = slice(s * width, (s + 1) * width)
        hi, lo = split2(jnp.transpose(buf[0, s, 0:emb, :]) * (0.5 / math.sqrt(emb)))
        ll[rs, 0:emb] = hi
        ll[rs, emb : 2 * emb] = hi
        ll[rs, 2 * emb : 3 * emb] = lo
        q = buf[0, s, emb + 3 : emb + 4, :] * buf[0, s, emb + 11 : emb + 12, :] * valid
        one = jnp.ones_like(q)
        m = jnp.concatenate([(q - 1.0) * HIDE, one, jnp.zeros((LANE - 2, width), f32)], 0)
        ll[rs, 3 * emb :] = jnp.transpose(m).astype(bf16)
        for f in range(2):
            p = [
                buf[0, s, emb + 8 * f + c : emb + 8 * f + c + 1, :] - mid[8 * f + c : 8 * f + c + 1, 0:1]
                for c in range(3)
            ]
            out = []
            for c in range(3):
                h, mm, l = pieces(p[c])
                out += [-2.0 * h, -2.0 * h, -2.0 * mm, -2.0 * mm, -2.0 * h, -2.0 * l]
            n = p[0] * p[0] + p[1] * p[1] + p[2] * p[2] + 1.0
            out += list(pieces(n)) + [one, one, one, jnp.zeros((LANE - 24, width), f32)]
            ld[f, rs, :] = jnp.transpose(jnp.concatenate(out, 0)).astype(bf16)[:, 0:32]
            tp[f, rs, :] = jnp.transpose(jnp.concatenate(p + [jnp.zeros((LANE - 3, width), f32)], 0))


def dot_piece(k, n0, n1, u, r0, R, rhs, rd, ll, ld, sc):
    ns = slice(n0, n1)
    rows = slice(r0, r0 + R)
    if k == 0:
        sc[0][:, ns] = jnp.dot(ll[rows, :], rhs[u, :, ns], preferred_element_type=f32)
    else:
        sc[k][:, ns] = jnp.dot(ld[k - 1, rows, :], rd[u, k - 1, :, ns], preferred_element_type=f32)


def strip(s, u, r0, cols, width, pc, acc, en, energy, sc):
    xs, d0s, d1s, gs = sc
    R = xs.shape[0]
    at = slice(r0 + s, r0 + s + 16)
    A = [acc[k, at, :] for k in range(8)]
    es = en[...] if energy else None
    for c0 in range(cols[0], cols[1], 256):
        c1 = min(c0 + 256, cols[1])
        cs = slice(c0, c1)
        x, a0, a1 = xs[s : s + 16, cs], d0s[s : s + 16, cs], d1s[s : s + 16, cs]
        q0, q1 = lax.rsqrt(a0), lax.rsqrt(a1)
        ch = a1 * q1 - a0 * q0
        v = jnp.tanh(x) * ch
        h = ch + v
        g = h * (ch - v)
        hi = g.astype(bf16)
        gs[s : s + 16, cs] = hi
        gs[R + s : R + s + 16, cs] = (g - hi.astype(f32)).astype(bf16)
        e = h * ch if energy else None
        w = (h * q0, h * q1)
        for k in range(0, c1 - c0, LANE):
            j = c0 + k
            side, js = j // width, slice(j % width, j % width + LANE)
            for f in range(2):
                wk = w[f][:, k : k + LANE]
                A[4 * f] = A[4 * f] + wk
                for c in range(3):
                    A[4 * f + 1 + c] = A[4 * f + 1 + c] + wk * pc[u, side, 8 * f + c : 8 * f + c + 1, js]
            if energy:
                es = es + (e[0:8, k : k + LANE] + e[8:16, k : k + LANE])
    for k in range(8):
        acc[k, at, :] = A[k]
    if energy:
        en[...] = es


def grad_dot(u, r0, cols, emb, rhs, ge, sc):
    R = sc[0].shape[0]
    cs = slice(*cols)
    o = lax.dot_general(
        sc[3][:, cs], rhs[u, 0 : 2 * emb, cs], (((1,), (1,)), ((), ())), preferred_element_type=f32
    )
    rows = slice(r0, r0 + R)
    ge[rows, :] = ge[rows, :] + ((o[:R, :emb] + o[:R, emb:]) + o[R:, :emb])


def tiles(jobs, energy, emb, width, pc, rhs, rd, ll, ld, scs, acc, ge, en):
    R = scs[0][0].shape[0]
    cols = (0, 2 * width)
    parts = [(k, n, n + 256) for n in range(0, 2 * width, 256) for k in range(3)]
    strips = list(range(0, R, 16))
    for part in parts:
        dot_piece(*part, jobs[0][1], jobs[0][0], R, rhs, rd, ll, ld, scs[0])
    for i, (r0, u) in enumerate(jobs):
        later = list(parts) if i + 1 < len(jobs) else []
        per = -(-len(later) // len(strips))
        for j, s in enumerate(strips):
            strip(s, u, r0, cols, width, pc, acc, en, energy, scs[i % NBUF])
            if j == 0 and i > 0:
                grad_dot(jobs[i - 1][1], jobs[i - 1][0], cols, emb, rhs, ge, scs[(i - 1) % NBUF])
            for _ in range(per):
                if later:
                    dot_piece(*later.pop(0), jobs[i + 1][1], jobs[i + 1][0], R, rhs, rd, ll, ld, scs[(i + 1) % NBUF])
    grad_dot(jobs[-1][1], jobs[-1][0], cols, emb, rhs, ge, scs[(len(jobs) - 1) % NBUF])


def finish(sides, weight, emb, width, acc, ge, tp, gres, pres):
    for s in sides:
        rs = slice(s * width, (s + 1) * width)
        gres[s] = jnp.transpose(ge[rs, :]) * (weight / (4.0 * math.sqrt(emb)))
        cols = lax.broadcasted_iota(jnp.int32, (width, LANE), 1)
        for f in range(2):
            ss = jnp.sum(acc[4 * f, rs, :], axis=1, keepdims=True)
            tt = jnp.zeros((width, LANE), f32)
            for c in range(3):
                tc = jnp.sum(acc[4 * f + 1 + c, rs, :], axis=1, keepdims=True)
                tt = tt + jnp.where(cols == c, tc, 0.0)
            res = (ss * tp[f, rs, :] - tt) * (weight if f else -weight)
            pres[s, f] = jnp.transpose(res)[0:8, :]


def kernel(
    R, emb, width, tracks, frames,
    pos, emb_in, vis, gpos, gemb, lout,
    pos_v, vis_v, e_ref, pm_ref, sin, buf, pc, mid, rhs, rd, ll, ld, tp, acc, ge, en, ent, gres, pres, prec, l1, l2,
    *rest,
):
    scs = [rest[4 * i : 4 * i + 4] for i in range(NBUF)]
    r1, s1, rg, sg, rr, sr, rl, sl = rest[4 * NBUF :]
    weight = rigidity / math.sqrt(tracks)
    n_track, n_tm = 16, 16
    track, tm = lax.axis_index("track"), lax.axis_index("tm")
    z, xl = track // 2, lax.rem(track, 2)
    plane, core = tm // 2, lax.rem(tm, 2)
    step = z // 2

    cur_to, next_to = [], []
    for l in range(2):
        f = 2 * core + l
        dz, slot, other = owner(z, f)
        cur_to.append((2 * dz + xl, 2 * plane + flip(core, other), slot))
        s = lax.rem(f + STEPS - 1, STEPS)
        back = jnp.where(f == 0, 1, 0)
        dz, slot, other = owner(z, s)
        next_to.append((2 * dz + xl, 2 * lax.rem(plane + PLANES - back, PLANES) + flip(s // 2, other), slot))
    home = step // 2
    mine = flip(core, home)
    sign = 2 * lax.rem(z, 2) - 1
    last = jnp.where(step == STEPS - 1, 1, 0)
    n_frame = lax.rem(step + 1, STEPS)
    n_tmid = 2 * lax.rem(plane + last, PLANES) + n_frame // 2
    cur_of, next_of = [], []
    for s in range(2):
        away = mine if s == 0 else 3 - mine
        zt = 2 * lax.rem(z + sign * away + ROWS, ROWS) + xl
        cur_of.append((zt, 2 * plane + home))
        next_of.append((zt, n_tmid))

    barrier = pltpu.get_barrier_semaphore()

    def greet(t, m):
        other = (t != track) | (m != tm)

        @pl.when(other)
        def _():
            pl.semaphore_signal(barrier, inc=1, device_id=(t, m), device_id_type=MESH)

        return jnp.where(other, 1, 0)

    met = n_track - 1 + n_tm - 1
    for t, m, _ in cur_to + next_to:
        met = met + greet(t, m)
    for t, m in cur_of + next_of:
        met = met + greet(t, m)
    for k in range(1, n_track):
        pl.semaphore_signal(barrier, inc=1, device_id=(lax.rem(track + k, n_track), tm), device_id_type=MESH)
    for k in range(1, n_tm):
        pl.semaphore_signal(barrier, inc=1, device_id=(track, lax.rem(tm + k, n_tm)), device_id_type=MESH)

    bring = [
        pltpu.make_async_copy(pos, pos_v, sin.at[0]),
        pltpu.make_async_copy(vis, vis_v, sin.at[1]),
        pltpu.make_async_copy(emb_in, e_ref, sin.at[2]),
    ]
    for c in bring:
        c.start()
    acc[...] = jnp.zeros_like(acc)
    ge[...] = jnp.zeros_like(ge)
    en[...] = jnp.zeros_like(en)
    ent[...] = jnp.zeros_like(ent)
    for c in bring:
        c.wait()
    for l in range(2):
        rows = [pos_v[c, l : l + 1, :] for c in range(3)] + [vis_v[l : l + 1, :].astype(f32)]
        pm_ref[l] = jnp.concatenate(rows + [jnp.zeros((4, width), f32)], 0)
    pl.semaphore_wait(barrier, met)

    def send(src, dst, ssem, rsem, t, m, start=True):
        same = (t == track) & (m == tm)
        if start:

            @pl.when(same)
            def _():
                pltpu.make_async_copy(src, dst, rsem).start()

        @pl.when(jnp.logical_not(same))
        def _():
            there = pltpu.make_async_remote_copy(
                src_ref=src, dst_ref=dst, send_sem=ssem, recv_sem=rsem, device_id=(t, m), device_id_type=MESH
            )
            there.start() if start else there.wait_send()

    def arrive(ref, sem):
        pltpu.make_async_copy(ref, ref, sem).wait()

    def stage1(start):
        for l in range(2):
            t, m, slot = cur_to[l]
            tn, mn, slot_n = next_to[l]
            send(pm_ref.at[l], buf.at[0, slot, pl.ds(emb, 8)], s1.at[0, l], r1.at[0, slot], t, m, start)
            send(pm_ref.at[l], buf.at[0, slot_n, pl.ds(emb + 8, 8)], s1.at[1, l], r1.at[1, slot_n], tn, mn, start)

    def stage1_emb(slots, start):
        for l in range(2):
            t, m, slot = cur_to[l]

            def go():
                send(e_ref.at[l], buf.at[0, slot, pl.ds(0, emb)], s1.at[2, l], r1.at[2, slot], t, m, start)

            if slots is None:
                go()
            else:
                pl.when(slot == slots)(go)

    peers = {
        1: (track, flip(core, 1) + 2 * plane),
        2: (2 * z + 1 - xl, tm),
        4: (2 * (z - sign * 1) + xl, tm),
    }

    def pass_on(n, src, dst, slot, via):
        t, m = peers[via]
        return pltpu.make_async_remote_copy(
            src_ref=buf.at[src, slot], dst_ref=buf.at[dst, slot], send_sem=sg.at[n], recv_sem=rg.at[dst, slot],
            device_id=(t, m), device_id_type=MESH,
        )

    first = [[pass_on(3 * s + k, 0, v, s, v) for k, v in enumerate((2, 4, 1))] for s in range(2)]
    second = [pass_on(6 + s, 2, 3, s, 1) for s in range(2)] + [pass_on(8 + s, 4, 5, s, 1) for s in range(2)]
    across = [pass_on(10, 2, 6, 0, 4), pass_on(11, 4, 6, 1, 2)]
    third = [pass_on(12 + s, 6, 7, s, 1) for s in range(2)]

    stage1_emb(0, True)
    stage1(True)
    valid = jnp.where((plane == PLANES - 1) & (step == STEPS - 1), 0.0, 1.0)

    def own(s):
        arrive(buf.at[0, s, pl.ds(emb, 8)], r1.at[0, s])
        arrive(buf.at[0, s, pl.ds(emb + 8, 8)], r1.at[1, s])
        arrive(buf.at[0, s, pl.ds(0, emb)], r1.at[2, s])
        for c in first[s]:
            c.start()
        prep_rows((s,), valid, emb, width, buf, mid, ll, ld, tp)

    def landed(u, s):
        arrive(buf.at[u, s], rg.at[u, s])

    own(0)

    def stage3(s, start):
        t, m = cur_of[s]
        tn, mn = next_of[s]
        l = lax.rem(step, 2)
        ln = lax.rem(n_frame, 2)
        send(gres.at[s], gemb.at[l], sr.at[2, s], rr.at[2, l], t, m, start)
        send(pres.at[s, 0], prec.at[l, 0], sr.at[0, s], rr.at[0, l], t, m, start)
        send(pres.at[s, 1], prec.at[ln, 1], sr.at[1, s], rr.at[1, ln], tn, mn, start)

    def round_of(n, group, here, size, send_at):
        return [
            pltpu.make_async_remote_copy(
                src_ref=group.at[here], dst_ref=group.at[here], send_sem=sl.at[n, k - 1], recv_sem=rl.at[n, here],
                device_id=send_at(lax.rem(here + k, size)), device_id_type=MESH,
            )
            for k in range(1, size)
        ]

    def gathered(n, group, here, size):
        for k in range(1, size):
            at = lax.rem(here + k, size)
            arrive(group.at[at], rl.at[n, at])

    cols = (emb, width, buf, pc, mid, rhs, rd)
    work = (emb, width, pc, rhs, rd, ll, ld, scs, acc, ge, en)

    @pl.loop(0, 4)
    def _(chip):
        @pl.when(chip == 0)
        def _():
            landed(1, 0)
            stage1_emb(1, True)

        @pl.when(chip == 1)
        def _():
            landed(2, 0)
            across[0].start()
            second[0].start()
            landed(4, 0)
            second[2].start()
            landed(3, 0)

        @pl.when(chip == 2)
        def _():
            landed(5, 0)

        @pl.when(chip == 3)
        def _():
            landed(6, 0)
            third[0].start()
            own(1)
            landed(7, 0)

        prep_cols(chip, 0, *cols)
        tiles([(0, 2 * chip)], True, *work)

    ent[...] = en[...]
    en[...] = jnp.zeros_like(en)

    @pl.loop(0, 4)
    def _(i):
        @pl.when(i == 1)
        def _():
            landed(2, 1)
            second[1].start()
            landed(4, 1)
            across[1].start()
            second[3].start()

        @pl.when(i == 2)
        def _():
            landed(1, 1)
            landed(3, 1)
            prep_cols(0, 1, *cols)
            prep_cols(1, 1, *cols)
            ent[...] = ent[...] + 2.0 * en[...]
            en[...] = jnp.zeros_like(en)

        @pl.when(i == 3)
        def _():
            landed(6, 1)
            third[1].start()
            landed(5, 1)
            prep_cols(2, 1, *cols)
            landed(7, 1)
            prep_cols(3, 1, *cols)

        g = 4 * lax.rem(i, 2) + i // 2
        tiles([(width, g), (width, g + 2)], True, *work)

    l1[track] = ent[...] + en[...]
    finish((1,), weight, emb, width, acc, ge, tp, gres, pres)
    round1 = round_of(0, l1, track, n_track, lambda t: (t, tm))
    round2 = round_of(1, l2, tm, n_tm, lambda m: (track, m))
    for c in round1:
        c.start()
    stage3(1, True)

    @pl.loop(0, 2)
    def _(i):
        @pl.when(i == 1)
        def _():
            gathered(0, l1, track, n_track)
            l2[tm] = jnp.sum(l1[...], axis=0)
            for c in round2:
                c.start()

        tiles([(0, 4 * i + 1), (0, 4 * i + 3)], ENERGY, *work)

    finish((0,), weight, emb, width, acc, ge, tp, gres, pres)
    stage3(0, True)
    for l in range(2):
        arrive(prec.at[l, 0], rr.at[0, l])
        arrive(prec.at[l, 1], rr.at[1, l])
        for c in range(3):
            gpos[c, l : l + 1, :] = prec[l, 0, c : c + 1, :] + prec[l, 1, c : c + 1, :]
        arrive(gemb.at[l], rr.at[2, l])
    gathered(1, l2, tm, n_tm)
    pairs = tracks * (tracks - 1) / 2.0 * (frames - 1)
    total = jnp.sum(jnp.sum(jnp.sum(l2[...], axis=0), axis=0, keepdims=True), axis=1, keepdims=True)
    lout[...] = total * (0.25 / pairs)

    stage1(False)
    stage1_emb(None, False)
    for c in first[0] + first[1] + second + across + third + round1 + round2:
        c.wait_send()
    for s in range(2):
        stage3(s, False)


def on_device(positions, embeddings, visible):
    frames_local, emb, width = embeddings.shape
    tracks = width * lax.axis_size("track")
    frames = frames_local * lax.axis_size("tm")
    R = width
    C = 2 * width
    K = 3 * emb + LANE
    dma, vmem = pltpu.SemaphoreType.DMA, pltpu.VMEM
    scratch = [
        vmem((3, 2, width), f32),
        vmem((2, width), jnp.int32),
        vmem((2, emb, width), f32),
        vmem((2, 8, width), f32),
        dma((3,)),
        vmem((8, 2, emb + 16, width), f32),
        vmem((8, 2, 16, width), f32),
        vmem((16, LANE), f32),
        vmem((8, K, C), bf16),
        vmem((8, 2, 32, C), bf16),
        vmem((C, K), bf16),
        vmem((2, C, 32), bf16),
        vmem((2, C, LANE), f32),
        vmem((8, C, LANE), f32),
        vmem((C, emb), f32),
        vmem((8, LANE), f32),
        vmem((8, LANE), f32),
        vmem((2, emb, width), f32),
        vmem((2, 2, 8, width), f32),
        vmem((2, 2, 8, width), f32),
        vmem((16, 8, LANE), f32),
        vmem((16, 8, LANE), f32),
    ]
    for _ in range(NBUF):
        scratch += [vmem((R, C), f32)] * 3 + [vmem((2 * R, C), bf16)]
    scratch += [dma((3, 2)), dma((3, 2)), dma((8, 2)), dma((14,)), dma((3, 2)), dma((3, 2)), dma((2, 16)), dma((2, 15))]
    whole, there = pl.BlockSpec(memory_space=pltpu.VMEM), pl.BlockSpec(memory_space=pl.ANY)
    grad_pos, grad_emb, loss = pl.pallas_call(
        functools.partial(kernel, R, emb, width, tracks, frames),
        out_shape=[
            vmem((3, 2, width), f32),
            vmem((2, emb, width), f32),
            vmem((1, 1), f32),
        ],
        in_specs=[there] * 3,
        out_specs=[whole] * 3,
        scratch_shapes=scratch,
        compiler_params=pltpu.CompilerParams(
            collective_id=0, has_side_effects=True, vmem_limit_bytes=60 * 2**20
        ),
    )(positions, embeddings, visible)
    return (grad_pos, grad_emb, loss.reshape(()))


def solution(mesh):
    in_specs = (P(None, "tm", "track"), P("tm", None, "track"), P("tm", "track"))
    out_specs = (P(None, "tm", "track"), P("tm", None, "track"), P())
    return jax.shard_map(
        on_device, mesh=mesh, in_specs=in_specs, out_specs=out_specs, check_vma=False
    )
```

```python
import functools
import math

import jax
import jax.numpy as jnp
from jax import lax
from jax.experimental import pallas as pl
from jax.experimental.pallas import tpu as pltpu
from jax.sharding import PartitionSpec as P

f32, bf16 = jnp.float32, jnp.bfloat16
MESH = pl.DeviceIdType.MESH
rigidity = 4.0
HIDE = 2.0**20
LANE = 128
ENERGY = True
NBUF = 2

ROWS = 8
PLANES = 8
STEPS = 4


def owner(z, f):
    rel = lax.rem(z - 2 * f + 2 * ROWS, ROWS)
    upper = jnp.where((rel >= 1) & (rel <= 4), 1, 0)
    away = jnp.where(upper == 1, rel - 1, lax.rem(ROWS - rel, ROWS))
    other = jnp.where((away == 1) | (away == 2), 1, 0)
    slot = jnp.where(away >= 2, 1, 0)
    return 2 * f + upper, slot, other


def flip(core, other):
    return core + other - 2 * core * other


def split2(v):
    hi = v.astype(bf16)
    return hi, (v - hi.astype(f32)).astype(bf16)


def pieces(v):
    h = v.astype(bf16).astype(f32)
    m = (v - h).astype(bf16).astype(f32)
    return h, m, (v - h - m).astype(bf16).astype(f32)


def prep_cols(chip, s, emb, width, buf, pc, mid, rhs, rd):
    g = 2 * chip + s
    for half in range(2):
        u = 2 * chip + half
        cs = slice(half * width, (half + 1) * width)
        hi, lo = split2(buf[u, s, 0:emb, :])
        rhs[g, 0:emb, cs] = hi
        rhs[g, emb : 2 * emb, cs] = lo
        rhs[g, 2 * emb : 3 * emb, cs] = hi
        q = buf[u, s, emb + 3 : emb + 4, :] * buf[u, s, emb + 11 : emb + 12, :]
        rows = lax.broadcasted_iota(jnp.int32, (LANE, width), 0)
        m = jnp.where(rows == 0, 1.0, 0.0) + jnp.where(rows == 1, (q - 1.0) * HIDE, 0.0)
        rhs[g, 3 * emb :, cs] = m.astype(bf16)
        for f in range(2):
            p = [
                buf[u, s, emb + 8 * f + c : emb + 8 * f + c + 1, :] - mid[8 * f + c : 8 * f + c + 1, 0:1]
                for c in range(3)
            ]
            out = []
            for c in range(3):
                pc[g, half, 8 * f + c : 8 * f + c + 1, :] = p[c]
                h, mm, l = pieces(p[c])
                out += [h, mm, h, mm, l, h]
            n = p[0] * p[0] + p[1] * p[1] + p[2] * p[2]
            one = jnp.ones_like(n)
            out += [one, one, one] + list(pieces(n)) + [jnp.zeros((8, width), f32)]
            rd[g, f, :, cs] = jnp.concatenate(out, 0).astype(bf16)


def prep_rows(sides, valid, emb, width, buf, mid, ll, ld, tp):
    if 0 in sides:
        mean = jnp.sum(buf[0, 0, emb:, :], 1, keepdims=True) / width
        mid[...] = jnp.broadcast_to(mean, mid.shape)
    for s in sides:
        rs = slice(s * width, (s + 1) * width)
        hi, lo = split2(jnp.transpose(buf[0, s, 0:emb, :]) * (0.5 / math.sqrt(emb)))
        ll[rs, 0:emb] = hi
        ll[rs, emb : 2 * emb] = hi
        ll[rs, 2 * emb : 3 * emb] = lo
        q = buf[0, s, emb + 3 : emb + 4, :] * buf[0, s, emb + 11 : emb + 12, :] * valid
        one = jnp.ones_like(q)
        m = jnp.concatenate([(q - 1.0) * HIDE, one, jnp.zeros((LANE - 2, width), f32)], 0)
        ll[rs, 3 * emb :] = jnp.transpose(m).astype(bf16)
        for f in range(2):
            p = [
                buf[0, s, emb + 8 * f + c : emb + 8 * f + c + 1, :] - mid[8 * f + c : 8 * f + c + 1, 0:1]
                for c in range(3)
            ]
            out = []
            for c in range(3):
                h, mm, l = pieces(p[c])
                out += [-2.0 * h, -2.0 * h, -2.0 * mm, -2.0 * mm, -2.0 * h, -2.0 * l]
            n = p[0] * p[0] + p[1] * p[1] + p[2] * p[2] + 1.0
            out += list(pieces(n)) + [one, one, one, jnp.zeros((LANE - 24, width), f32)]
            ld[f, rs, :] = jnp.transpose(jnp.concatenate(out, 0)).astype(bf16)[:, 0:32]
            tp[f, rs, :] = jnp.transpose(jnp.concatenate(p + [jnp.zeros((LANE - 3, width), f32)], 0))


def dot_piece(k, n0, n1, u, r0, R, rhs, rd, ll, ld, sc):
    ns = slice(n0, n1)
    rows = slice(r0, r0 + R)
    if k == 0:
        sc[0][:, ns] = jnp.dot(ll[rows, :], rhs[u, :, ns], preferred_element_type=f32)
    else:
        sc[k][:, ns] = jnp.dot(ld[k - 1, rows, :], rd[u, k - 1, :, ns], preferred_element_type=f32)


def strip(s, u, r0, cols, width, pc, acc, en, energy, sc):
    xs, d0s, d1s, gs = sc
    R = xs.shape[0]
    at = slice(r0 + s, r0 + s + 16)
    A = [acc[k, at, :] for k in range(8)]
    es = en[...] if energy else None
    for c0 in range(cols[0], cols[1], 256):
        c1 = min(c0 + 256, cols[1])
        cs = slice(c0, c1)
        x, a0, a1 = xs[s : s + 16, cs], d0s[s : s + 16, cs], d1s[s : s + 16, cs]
        q0, q1 = lax.rsqrt(a0), lax.rsqrt(a1)
        ch = a1 * q1 - a0 * q0
        v = jnp.tanh(x) * ch
        h = ch + v
        g = h * (ch - v)
        hi = g.astype(bf16)
        gs[s : s + 16, cs] = hi
        gs[R + s : R + s + 16, cs] = (g - hi.astype(f32)).astype(bf16)
        e = h * ch if energy else None
        w = (h * q0, h * q1)
        for k in range(0, c1 - c0, LANE):
            j = c0 + k
            side, js = j // width, slice(j % width, j % width + LANE)
            for f in range(2):
                wk = w[f][:, k : k + LANE]
                A[4 * f] = A[4 * f] + wk
                for c in range(3):
                    A[4 * f + 1 + c] = A[4 * f + 1 + c] + wk * pc[u, side, 8 * f + c : 8 * f + c + 1, js]
            if energy:
                es = es + (e[0:8, k : k + LANE] + e[8:16, k : k + LANE])
    for k in range(8):
        acc[k, at, :] = A[k]
    if energy:
        en[...] = es


def grad_dot(u, r0, cols, emb, rhs, ge, sc):
    R = sc[0].shape[0]
    cs = slice(*cols)
    o = lax.dot_general(
        sc[3][:, cs], rhs[u, 0 : 2 * emb, cs], (((1,), (1,)), ((), ())), preferred_element_type=f32
    )
    rows = slice(r0, r0 + R)
    ge[rows, :] = ge[rows, :] + ((o[:R, :emb] + o[:R, emb:]) + o[R:, :emb])


def tiles(jobs, energy, emb, width, pc, rhs, rd, ll, ld, scs, acc, ge, en):
    R = scs[0][0].shape[0]
    cols = (0, 2 * width)
    parts = [(k, n, n + 256) for n in range(0, 2 * width, 256) for k in range(3)]
    strips = list(range(0, R, 16))
    for part in parts:
        dot_piece(*part, jobs[0][1], jobs[0][0], R, rhs, rd, ll, ld, scs[0])
    for i, (r0, u) in enumerate(jobs):
        later = list(parts) if i + 1 < len(jobs) else []
        per = -(-len(later) // len(strips))
        for j, s in enumerate(strips):
            strip(s, u, r0, cols, width, pc, acc, en, energy, scs[i % NBUF])
            if j == 0 and i > 0:
                grad_dot(jobs[i - 1][1], jobs[i - 1][0], cols, emb, rhs, ge, scs[(i - 1) % NBUF])
            for _ in range(per):
                if later:
                    dot_piece(*later.pop(0), jobs[i + 1][1], jobs[i + 1][0], R, rhs, rd, ll, ld, scs[(i + 1) % NBUF])
    grad_dot(jobs[-1][1], jobs[-1][0], cols, emb, rhs, ge, scs[(len(jobs) - 1) % NBUF])


def finish(sides, weight, emb, width, acc, ge, tp, gres, pres):
    for s in sides:
        rs = slice(s * width, (s + 1) * width)
        gres[s] = jnp.transpose(ge[rs, :]) * (weight / (4.0 * math.sqrt(emb)))
        cols = lax.broadcasted_iota(jnp.int32, (width, LANE), 1)
        for f in range(2):
            ss = jnp.sum(acc[4 * f, rs, :], axis=1, keepdims=True)
            tt = jnp.zeros((width, LANE), f32)
            for c in range(3):
                tc = jnp.sum(acc[4 * f + 1 + c, rs, :], axis=1, keepdims=True)
                tt = tt + jnp.where(cols == c, tc, 0.0)
            res = (ss * tp[f, rs, :] - tt) * (weight if f else -weight)
            pres[s, f] = jnp.transpose(res)[0:8, :]


def kernel(
    R, emb, width, tracks, frames,
    pos, emb_in, vis, gpos, gemb, lout,
    pos_v, vis_v, e_ref, pm_ref, sin, buf, pc, mid, rhs, rd, ll, ld, tp, acc, ge, en, ent, gres, pres, prec, l1, l2,
    *rest,
):
    scs = [rest[4 * i : 4 * i + 4] for i in range(NBUF)]
    r1, s1, rg, sg, rr, sr, rl, sl = rest[4 * NBUF :]
    weight = rigidity / math.sqrt(tracks)
    n_track, n_tm = 16, 16
    track, tm = lax.axis_index("track"), lax.axis_index("tm")
    z, xl = track // 2, lax.rem(track, 2)
    plane, core = tm // 2, lax.rem(tm, 2)
    step = z // 2

    cur_to, next_to = [], []
    for l in range(2):
        f = 2 * core + l
        dz, slot, other = owner(z, f)
        cur_to.append((2 * dz + xl, 2 * plane + flip(core, other), slot))
        s = lax.rem(f + STEPS - 1, STEPS)
        back = jnp.where(f == 0, 1, 0)
        dz, slot, other = owner(z, s)
        next_to.append((2 * dz + xl, 2 * lax.rem(plane + PLANES - back, PLANES) + flip(s // 2, other), slot))
    home = step // 2
    mine = flip(core, home)
    sign = 2 * lax.rem(z, 2) - 1
    last = jnp.where(step == STEPS - 1, 1, 0)
    n_frame = lax.rem(step + 1, STEPS)
    n_tmid = 2 * lax.rem(plane + last, PLANES) + n_frame // 2
    cur_of, next_of = [], []
    for s in range(2):
        away = mine if s == 0 else 3 - mine
        zt = 2 * lax.rem(z + sign * away + ROWS, ROWS) + xl
        cur_of.append((zt, 2 * plane + home))
        next_of.append((zt, n_tmid))

    barrier = pltpu.get_barrier_semaphore()

    def greet(t, m):
        other = (t != track) | (m != tm)

        @pl.when(other)
        def _():
            pl.semaphore_signal(barrier, inc=1, device_id=(t, m), device_id_type=MESH)

        return jnp.where(other, 1, 0)

    met = n_track - 1 + n_tm - 1
    for t, m, _ in cur_to + next_to:
        met = met + greet(t, m)
    for t, m in cur_of + next_of:
        met = met + greet(t, m)
    for k in range(1, n_track):
        pl.semaphore_signal(barrier, inc=1, device_id=(lax.rem(track + k, n_track), tm), device_id_type=MESH)
    for k in range(1, n_tm):
        pl.semaphore_signal(barrier, inc=1, device_id=(track, lax.rem(tm + k, n_tm)), device_id_type=MESH)

    bring = [
        pltpu.make_async_copy(pos, pos_v, sin.at[0]),
        pltpu.make_async_copy(vis, vis_v, sin.at[1]),
        pltpu.make_async_copy(emb_in, e_ref, sin.at[2]),
    ]
    for c in bring:
        c.start()
    acc[...] = jnp.zeros_like(acc)
    ge[...] = jnp.zeros_like(ge)
    en[...] = jnp.zeros_like(en)
    ent[...] = jnp.zeros_like(ent)
    for c in bring:
        c.wait()
    for l in range(2):
        rows = [pos_v[c, l : l + 1, :] for c in range(3)] + [vis_v[l : l + 1, :].astype(f32)]
        pm_ref[l] = jnp.concatenate(rows + [jnp.zeros((4, width), f32)], 0)
    pl.semaphore_wait(barrier, met)

    def send(src, dst, ssem, rsem, t, m, start=True):
        same = (t == track) & (m == tm)
        if start:

            @pl.when(same)
            def _():
                pltpu.make_async_copy(src, dst, rsem).start()

        @pl.when(jnp.logical_not(same))
        def _():
            there = pltpu.make_async_remote_copy(
                src_ref=src, dst_ref=dst, send_sem=ssem, recv_sem=rsem, device_id=(t, m), device_id_type=MESH
            )
            there.start() if start else there.wait_send()

    def arrive(ref, sem):
        pltpu.make_async_copy(ref, ref, sem).wait()

    def stage1(start):
        for l in range(2):
            t, m, slot = cur_to[l]
            tn, mn, slot_n = next_to[l]
            send(pm_ref.at[l], buf.at[0, slot, pl.ds(emb, 8)], s1.at[0, l], r1.at[0, slot], t, m, start)
            send(pm_ref.at[l], buf.at[0, slot_n, pl.ds(emb + 8, 8)], s1.at[1, l], r1.at[1, slot_n], tn, mn, start)

    def stage1_emb(slots, start):
        for l in range(2):
            t, m, slot = cur_to[l]

            def go():
                send(e_ref.at[l], buf.at[0, slot, pl.ds(0, emb)], s1.at[2, l], r1.at[2, slot], t, m, start)

            if slots is None:
                go()
            else:
                pl.when(slot == slots)(go)

    peers = {
        1: (track, flip(core, 1) + 2 * plane),
        2: (2 * z + 1 - xl, tm),
        4: (2 * (z - sign * 1) + xl, tm),
    }

    def pass_on(n, src, dst, slot, via):
        t, m = peers[via]
        return pltpu.make_async_remote_copy(
            src_ref=buf.at[src, slot], dst_ref=buf.at[dst, slot], send_sem=sg.at[n], recv_sem=rg.at[dst, slot],
            device_id=(t, m), device_id_type=MESH,
        )

    first = [[pass_on(3 * s + k, 0, v, s, v) for k, v in enumerate((2, 4, 1))] for s in range(2)]
    second = [pass_on(6 + s, 2, 3, s, 1) for s in range(2)] + [pass_on(8 + s, 4, 5, s, 1) for s in range(2)]
    across = [pass_on(10, 2, 6, 0, 4), pass_on(11, 4, 6, 1, 2)]
    third = [pass_on(12 + s, 6, 7, s, 1) for s in range(2)]

    stage1(True)
    stage1_emb(0, True)
    valid = jnp.where((plane == PLANES - 1) & (step == STEPS - 1), 0.0, 1.0)

    def own(s):
        arrive(buf.at[0, s, pl.ds(emb, 8)], r1.at[0, s])
        arrive(buf.at[0, s, pl.ds(emb + 8, 8)], r1.at[1, s])
        arrive(buf.at[0, s, pl.ds(0, emb)], r1.at[2, s])
        for c in first[s]:
            c.start()
        prep_rows((s,), valid, emb, width, buf, mid, ll, ld, tp)

    def landed(u, s):
        arrive(buf.at[u, s], rg.at[u, s])

    own(0)

    def stage3(s, start):
        t, m = cur_of[s]
        tn, mn = next_of[s]
        l = lax.rem(step, 2)
        ln = lax.rem(n_frame, 2)
        send(gres.at[s], gemb.at[l], sr.at[2, s], rr.at[2, l], t, m, start)
        send(pres.at[s, 0], prec.at[l, 0], sr.at[0, s], rr.at[0, l], t, m, start)
        send(pres.at[s, 1], prec.at[ln, 1], sr.at[1, s], rr.at[1, ln], tn, mn, start)

    def round_of(n, group, here, size, send_at):
        return [
            pltpu.make_async_remote_copy(
                src_ref=group.at[here], dst_ref=group.at[here], send_sem=sl.at[n, k - 1], recv_sem=rl.at[n, here],
                device_id=send_at(lax.rem(here + k, size)), device_id_type=MESH,
            )
            for k in range(1, size)
        ]

    def gathered(n, group, here, size):
        for k in range(1, size):
            at = lax.rem(here + k, size)
            arrive(group.at[at], rl.at[n, at])

    cols = (emb, width, buf, pc, mid, rhs, rd)
    work = (emb, width, pc, rhs, rd, ll, ld, scs, acc, ge, en)

    @pl.loop(0, 3)
    def _(chip):
        @pl.when(chip == 0)
        def _():
            landed(1, 0)
            stage1_emb(1, True)

        @pl.when(chip == 1)
        def _():
            landed(2, 0)
            across[0].start()
            second[0].start()
            landed(4, 0)
            second[2].start()
            landed(3, 0)

        @pl.when(chip == 2)
        def _():
            landed(5, 0)

        prep_cols(chip, 0, *cols)
        tiles([(0, 2 * chip)], True, *work)

    ent[...] = en[...]
    en[...] = jnp.zeros_like(en)
    own(1)
    landed(6, 0)
    third[0].start()

    @pl.loop(0, 4)
    def _(i):
        @pl.when(i == 1)
        def _():
            landed(7, 0)
            prep_cols(3, 0, *cols)
            ent[...] = ent[...] + 2.0 * en[...]
            en[...] = jnp.zeros_like(en)
            tiles([(0, 6)], True, *work)
            ent[...] = ent[...] + en[...]
            en[...] = jnp.zeros_like(en)
            landed(2, 1)
            second[1].start()
            landed(4, 1)
            across[1].start()
            second[3].start()

        @pl.when(i == 2)
        def _():
            landed(1, 1)
            landed(3, 1)
            prep_cols(0, 1, *cols)
            prep_cols(1, 1, *cols)
            ent[...] = ent[...] + 2.0 * en[...]
            en[...] = jnp.zeros_like(en)

        @pl.when(i == 3)
        def _():
            landed(6, 1)
            third[1].start()
            landed(5, 1)
            prep_cols(2, 1, *cols)
            landed(7, 1)
            prep_cols(3, 1, *cols)

        g = 4 * lax.rem(i, 2) + i // 2
        tiles([(width, g), (width, g + 2)], True, *work)

    l1[track] = ent[...] + en[...]
    finish((1,), weight, emb, width, acc, ge, tp, gres, pres)
    round1 = round_of(0, l1, track, n_track, lambda t: (t, tm))
    round2 = round_of(1, l2, tm, n_tm, lambda m: (track, m))
    for c in round1:
        c.start()
    stage3(1, True)

    @pl.loop(0, 2)
    def _(i):
        @pl.when(i == 1)
        def _():
            gathered(0, l1, track, n_track)
            l2[tm] = jnp.sum(l1[...], axis=0)
            for c in round2:
                c.start()

        tiles([(0, 4 * i + 1), (0, 4 * i + 3)], ENERGY, *work)

    finish((0,), weight, emb, width, acc, ge, tp, gres, pres)
    stage3(0, True)
    for l in range(2):
        arrive(prec.at[l, 0], rr.at[0, l])
        arrive(prec.at[l, 1], rr.at[1, l])
        for c in range(3):
            gpos[c, l : l + 1, :] = prec[l, 0, c : c + 1, :] + prec[l, 1, c : c + 1, :]
        arrive(gemb.at[l], rr.at[2, l])
    gathered(1, l2, tm, n_tm)
    pairs = tracks * (tracks - 1) / 2.0 * (frames - 1)
    total = jnp.sum(jnp.sum(jnp.sum(l2[...], axis=0), axis=0, keepdims=True), axis=1, keepdims=True)
    lout[...] = total * (0.25 / pairs)

    stage1(False)
    stage1_emb(None, False)
    for c in first[0] + first[1] + second + across + third + round1 + round2:
        c.wait_send()
    for s in range(2):
        stage3(s, False)


def on_device(positions, embeddings, visible):
    frames_local, emb, width = embeddings.shape
    tracks = width * lax.axis_size("track")
    frames = frames_local * lax.axis_size("tm")
    R = width
    C = 2 * width
    K = 3 * emb + LANE
    dma, vmem = pltpu.SemaphoreType.DMA, pltpu.VMEM
    scratch = [
        vmem((3, 2, width), f32),
        vmem((2, width), jnp.int32),
        vmem((2, emb, width), f32),
        vmem((2, 8, width), f32),
        dma((3,)),
        vmem((8, 2, emb + 16, width), f32),
        vmem((8, 2, 16, width), f32),
        vmem((16, LANE), f32),
        vmem((8, K, C), bf16),
        vmem((8, 2, 32, C), bf16),
        vmem((C, K), bf16),
        vmem((2, C, 32), bf16),
        vmem((2, C, LANE), f32),
        vmem((8, C, LANE), f32),
        vmem((C, emb), f32),
        vmem((8, LANE), f32),
        vmem((8, LANE), f32),
        vmem((2, emb, width), f32),
        vmem((2, 2, 8, width), f32),
        vmem((2, 2, 8, width), f32),
        vmem((16, 8, LANE), f32),
        vmem((16, 8, LANE), f32),
    ]
    for _ in range(NBUF):
        scratch += [vmem((R, C), f32)] * 3 + [vmem((2 * R, C), bf16)]
    scratch += [dma((3, 2)), dma((3, 2)), dma((8, 2)), dma((14,)), dma((3, 2)), dma((3, 2)), dma((2, 16)), dma((2, 15))]
    whole, there = pl.BlockSpec(memory_space=pltpu.VMEM), pl.BlockSpec(memory_space=pl.ANY)
    grad_pos, grad_emb, loss = pl.pallas_call(
        functools.partial(kernel, R, emb, width, tracks, frames),
        out_shape=[
            vmem((3, 2, width), f32),
            vmem((2, emb, width), f32),
            vmem((1, 1), f32),
        ],
        in_specs=[there] * 3,
        out_specs=[whole] * 3,
        scratch_shapes=scratch,
        compiler_params=pltpu.CompilerParams(
            collective_id=0, has_side_effects=True, vmem_limit_bytes=60 * 2**20
        ),
    )(positions, embeddings, visible)
    return (grad_pos, grad_emb, loss.reshape(()))


def solution(mesh):
    in_specs = (P(None, "tm", "track"), P("tm", None, "track"), P("tm", "track"))
    out_specs = (P(None, "tm", "track"), P("tm", None, "track"), P())
    return jax.shard_map(
        on_device, mesh=mesh, in_specs=in_specs, out_specs=out_specs, check_vma=False
    )
```

```python
import functools
import math

import jax
import jax.numpy as jnp
from jax import lax
from jax.experimental import pallas as pl
from jax.experimental.pallas import tpu as pltpu
from jax.sharding import PartitionSpec as P

f32, bf16 = jnp.float32, jnp.bfloat16
MESH = pl.DeviceIdType.MESH
rigidity = 4.0
HIDE = 2.0**20
LANE = 128
ENERGY = True
NBUF = 2

ROWS = 8
PLANES = 8
STEPS = 4


def owner(z, f):
    rel = lax.rem(z - 2 * f + 2 * ROWS, ROWS)
    upper = jnp.where((rel >= 1) & (rel <= 4), 1, 0)
    away = jnp.where(upper == 1, rel - 1, lax.rem(ROWS - rel, ROWS))
    other = jnp.where((away == 1) | (away == 2), 1, 0)
    slot = jnp.where(away >= 2, 1, 0)
    return 2 * f + upper, slot, other


def flip(core, other):
    return core + other - 2 * core * other


def split2(v):
    hi = v.astype(bf16)
    return hi, (v - hi.astype(f32)).astype(bf16)


def pieces(v):
    h = v.astype(bf16).astype(f32)
    m = (v - h).astype(bf16).astype(f32)
    return h, m, (v - h - m).astype(bf16).astype(f32)


def prep_cols(chip, s, emb, width, buf, pc, mid, rhs, rd):
    g = 2 * chip + s
    for half in range(2):
        u = 2 * chip + half
        cs = slice(half * width, (half + 1) * width)
        hi, lo = split2(buf[u, s, 0:emb, :])
        rhs[g, 0:emb, cs] = hi
        rhs[g, emb : 2 * emb, cs] = lo
        rhs[g, 2 * emb : 3 * emb, cs] = hi
        q = buf[u, s, emb + 3 : emb + 4, :] * buf[u, s, emb + 11 : emb + 12, :]
        rows = lax.broadcasted_iota(jnp.int32, (LANE, width), 0)
        m = jnp.where(rows == 0, 1.0, 0.0) + jnp.where(rows == 1, (q - 1.0) * HIDE, 0.0)
        rhs[g, 3 * emb :, cs] = m.astype(bf16)
        for f in range(2):
            p = [
                buf[u, s, emb + 8 * f + c : emb + 8 * f + c + 1, :] - mid[8 * f + c : 8 * f + c + 1, 0:1]
                for c in range(3)
            ]
            out = []
            for c in range(3):
                pc[g, half, 8 * f + c : 8 * f + c + 1, :] = p[c]
                h, mm, l = pieces(p[c])
                out += [h, mm, h, mm, l, h]
            n = p[0] * p[0] + p[1] * p[1] + p[2] * p[2]
            one = jnp.ones_like(n)
            out += [one, one, one] + list(pieces(n)) + [jnp.zeros((8, width), f32)]
            rd[g, f, :, cs] = jnp.concatenate(out, 0).astype(bf16)


def prep_rows(sides, valid, emb, width, buf, mid, ll, ld, tp):
    if 0 in sides:
        mean = jnp.sum(buf[0, 0, emb:, :], 1, keepdims=True) / width
        mid[...] = jnp.broadcast_to(mean, mid.shape)
    for s in sides:
        rs = slice(s * width, (s + 1) * width)
        hi, lo = split2(jnp.transpose(buf[0, s, 0:emb, :]) * (0.5 / math.sqrt(emb)))
        ll[rs, 0:emb] = hi
        ll[rs, emb : 2 * emb] = hi
        ll[rs, 2 * emb : 3 * emb] = lo
        q = buf[0, s, emb + 3 : emb + 4, :] * buf[0, s, emb + 11 : emb + 12, :] * valid
        one = jnp.ones_like(q)
        m = jnp.concatenate([(q - 1.0) * HIDE, one, jnp.zeros((LANE - 2, width), f32)], 0)
        ll[rs, 3 * emb :] = jnp.transpose(m).astype(bf16)
        for f in range(2):
            p = [
                buf[0, s, emb + 8 * f + c : emb + 8 * f + c + 1, :] - mid[8 * f + c : 8 * f + c + 1, 0:1]
                for c in range(3)
            ]
            out = []
            for c in range(3):
                h, mm, l = pieces(p[c])
                out += [-2.0 * h, -2.0 * h, -2.0 * mm, -2.0 * mm, -2.0 * h, -2.0 * l]
            n = p[0] * p[0] + p[1] * p[1] + p[2] * p[2] + 1.0
            out += list(pieces(n)) + [one, one, one, jnp.zeros((LANE - 24, width), f32)]
            ld[f, rs, :] = jnp.transpose(jnp.concatenate(out, 0)).astype(bf16)[:, 0:32]
            tp[f, rs, :] = jnp.transpose(jnp.concatenate(p + [jnp.zeros((LANE - 3, width), f32)], 0))


def dot_piece(k, n0, n1, u, r0, R, rhs, rd, ll, ld, sc):
    ns = slice(n0, n1)
    rows = slice(r0, r0 + R)
    if k == 0:
        sc[0][:, ns] = jnp.dot(ll[rows, :], rhs[u, :, ns], preferred_element_type=f32)
    else:
        sc[k][:, ns] = jnp.dot(ld[k - 1, rows, :], rd[u, k - 1, :, ns], preferred_element_type=f32)


def strip(s, u, r0, cols, width, pc, acc, en, energy, sc):
    xs, d0s, d1s, gs = sc
    R = xs.shape[0]
    at = slice(r0 + s, r0 + s + 16)
    A = [acc[k, at, :] for k in range(8)]
    es = en[...] if energy else None
    for c0 in range(cols[0], cols[1], 256):
        c1 = min(c0 + 256, cols[1])
        cs = slice(c0, c1)
        x, a0, a1 = xs[s : s + 16, cs], d0s[s : s + 16, cs], d1s[s : s + 16, cs]
        q0, q1 = lax.rsqrt(a0), lax.rsqrt(a1)
        ch = a1 * q1 - a0 * q0
        v = jnp.tanh(x) * ch
        h = ch + v
        g = h * (ch - v)
        hi = g.astype(bf16)
        gs[s : s + 16, cs] = hi
        gs[R + s : R + s + 16, cs] = (g - hi.astype(f32)).astype(bf16)
        e = h * ch if energy else None
        w = (h * q0, h * q1)
        for k in range(0, c1 - c0, LANE):
            j = c0 + k
            side, js = j // width, slice(j % width, j % width + LANE)
            for f in range(2):
                wk = w[f][:, k : k + LANE]
                A[4 * f] = A[4 * f] + wk
                for c in range(3):
                    A[4 * f + 1 + c] = A[4 * f + 1 + c] + wk * pc[u, side, 8 * f + c : 8 * f + c + 1, js]
            if energy:
                es = es + (e[0:8, k : k + LANE] + e[8:16, k : k + LANE])
    for k in range(8):
        acc[k, at, :] = A[k]
    if energy:
        en[...] = es


def grad_dot(u, r0, cols, emb, rhs, ge, sc):
    R = sc[0].shape[0]
    cs = slice(*cols)
    o = lax.dot_general(
        sc[3][:, cs], rhs[u, 0 : 2 * emb, cs], (((1,), (1,)), ((), ())), preferred_element_type=f32
    )
    rows = slice(r0, r0 + R)
    ge[rows, :] = ge[rows, :] + ((o[:R, :emb] + o[:R, emb:]) + o[R:, :emb])


def tiles(jobs, energy, emb, width, pc, rhs, rd, ll, ld, scs, acc, ge, en):
    R = scs[0][0].shape[0]
    cols = (0, 2 * width)
    parts = [(k, n, n + 256) for n in range(0, 2 * width, 256) for k in range(3)]
    strips = list(range(0, R, 16))
    for part in parts:
        dot_piece(*part, jobs[0][1], jobs[0][0], R, rhs, rd, ll, ld, scs[0])
    for i, (r0, u) in enumerate(jobs):
        later = list(parts) if i + 1 < len(jobs) else []
        per = -(-len(later) // len(strips))
        for j, s in enumerate(strips):
            strip(s, u, r0, cols, width, pc, acc, en, energy, scs[i % NBUF])
            if j == 0 and i > 0:
                grad_dot(jobs[i - 1][1], jobs[i - 1][0], cols, emb, rhs, ge, scs[(i - 1) % NBUF])
            for _ in range(per):
                if later:
                    dot_piece(*later.pop(0), jobs[i + 1][1], jobs[i + 1][0], R, rhs, rd, ll, ld, scs[(i + 1) % NBUF])
    grad_dot(jobs[-1][1], jobs[-1][0], cols, emb, rhs, ge, scs[(len(jobs) - 1) % NBUF])


def finish(sides, weight, emb, width, acc, ge, tp, gres, pres):
    for s in sides:
        rs = slice(s * width, (s + 1) * width)
        gres[s] = jnp.transpose(ge[rs, :]) * (weight / (4.0 * math.sqrt(emb)))
        cols = lax.broadcasted_iota(jnp.int32, (width, LANE), 1)
        for f in range(2):
            ss = jnp.sum(acc[4 * f, rs, :], axis=1, keepdims=True)
            tt = jnp.zeros((width, LANE), f32)
            for c in range(3):
                tc = jnp.sum(acc[4 * f + 1 + c, rs, :], axis=1, keepdims=True)
                tt = tt + jnp.where(cols == c, tc, 0.0)
            res = (ss * tp[f, rs, :] - tt) * (weight if f else -weight)
            pres[s, f] = jnp.transpose(res)[0:8, :]


def kernel(
    R, emb, width, tracks, frames,
    pos, emb_in, vis, gpos, gemb, lout,
    pos_v, vis_v, e_ref, pm_ref, sin, buf, pc, mid, rhs, rd, ll, ld, tp, acc, ge, en, ent, gres, pres, prec, l1, l2,
    *rest,
):
    scs = [rest[4 * i : 4 * i + 4] for i in range(NBUF)]
    r1, s1, rg, sg, rr, sr, rl, sl = rest[4 * NBUF :]
    weight = rigidity / math.sqrt(tracks)
    n_track, n_tm = 16, 16
    track, tm = lax.axis_index("track"), lax.axis_index("tm")
    z, xl = track // 2, lax.rem(track, 2)
    plane, core = tm // 2, lax.rem(tm, 2)
    step = z // 2

    cur_to, next_to = [], []
    for l in range(2):
        f = 2 * core + l
        dz, slot, other = owner(z, f)
        cur_to.append((2 * dz + xl, 2 * plane + flip(core, other), slot))
        s = lax.rem(f + STEPS - 1, STEPS)
        back = jnp.where(f == 0, 1, 0)
        dz, slot, other = owner(z, s)
        next_to.append((2 * dz + xl, 2 * lax.rem(plane + PLANES - back, PLANES) + flip(s // 2, other), slot))
    home = step // 2
    mine = flip(core, home)
    sign = 2 * lax.rem(z, 2) - 1
    last = jnp.where(step == STEPS - 1, 1, 0)
    n_frame = lax.rem(step + 1, STEPS)
    n_tmid = 2 * lax.rem(plane + last, PLANES) + n_frame // 2
    cur_of, next_of = [], []
    for s in range(2):
        away = mine if s == 0 else 3 - mine
        zt = 2 * lax.rem(z + sign * away + ROWS, ROWS) + xl
        cur_of.append((zt, 2 * plane + home))
        next_of.append((zt, n_tmid))

    barrier = pltpu.get_barrier_semaphore()

    def greet(t, m):
        other = (t != track) | (m != tm)

        @pl.when(other)
        def _():
            pl.semaphore_signal(barrier, inc=1, device_id=(t, m), device_id_type=MESH)

        return jnp.where(other, 1, 0)

    met = n_track - 1 + n_tm - 1
    for t, m, _ in cur_to + next_to:
        met = met + greet(t, m)
    for t, m in cur_of + next_of:
        met = met + greet(t, m)
    for k in range(1, n_track):
        pl.semaphore_signal(barrier, inc=1, device_id=(lax.rem(track + k, n_track), tm), device_id_type=MESH)
    for k in range(1, n_tm):
        pl.semaphore_signal(barrier, inc=1, device_id=(track, lax.rem(tm + k, n_tm)), device_id_type=MESH)

    bring = [
        pltpu.make_async_copy(pos, pos_v, sin.at[0]),
        pltpu.make_async_copy(vis, vis_v, sin.at[1]),
        pltpu.make_async_copy(emb_in, e_ref, sin.at[2]),
    ]
    for c in bring:
        c.start()
    acc[...] = jnp.zeros_like(acc)
    ge[...] = jnp.zeros_like(ge)
    en[...] = jnp.zeros_like(en)
    ent[...] = jnp.zeros_like(ent)
    for c in bring:
        c.wait()
    for l in range(2):
        rows = [pos_v[c, l : l + 1, :] for c in range(3)] + [vis_v[l : l + 1, :].astype(f32)]
        pm_ref[l] = jnp.concatenate(rows + [jnp.zeros((4, width), f32)], 0)
    pl.semaphore_wait(barrier, met)

    def send(src, dst, ssem, rsem, t, m, start=True):
        same = (t == track) & (m == tm)
        if start:

            @pl.when(same)
            def _():
                pltpu.make_async_copy(src, dst, rsem).start()

        @pl.when(jnp.logical_not(same))
        def _():
            there = pltpu.make_async_remote_copy(
                src_ref=src, dst_ref=dst, send_sem=ssem, recv_sem=rsem, device_id=(t, m), device_id_type=MESH
            )
            there.start() if start else there.wait_send()

    def arrive(ref, sem):
        pltpu.make_async_copy(ref, ref, sem).wait()

    def stage1(start):
        for l in range(2):
            t, m, slot = cur_to[l]
            tn, mn, slot_n = next_to[l]
            send(pm_ref.at[l], buf.at[0, slot, pl.ds(emb, 8)], s1.at[0, l], r1.at[0, slot], t, m, start)
            send(pm_ref.at[l], buf.at[0, slot_n, pl.ds(emb + 8, 8)], s1.at[1, l], r1.at[1, slot_n], tn, mn, start)

    def stage1_emb(slots, start):
        for l in range(2):
            t, m, slot = cur_to[l]

            def go():
                send(e_ref.at[l], buf.at[0, slot, pl.ds(0, emb)], s1.at[2, l], r1.at[2, slot], t, m, start)

            if slots is None:
                go()
            else:
                pl.when(slot == slots)(go)

    peers = {
        1: (track, flip(core, 1) + 2 * plane),
        2: (2 * z + 1 - xl, tm),
        4: (2 * (z - sign * 1) + xl, tm),
    }

    def pass_on(n, src, dst, slot, via):
        t, m = peers[via]
        return pltpu.make_async_remote_copy(
            src_ref=buf.at[src, slot], dst_ref=buf.at[dst, slot], send_sem=sg.at[n], recv_sem=rg.at[dst, slot],
            device_id=(t, m), device_id_type=MESH,
        )

    first = [[pass_on(3 * s + k, 0, v, s, v) for k, v in enumerate((2, 4, 1))] for s in range(2)]
    second = [pass_on(6 + s, 2, 3, s, 1) for s in range(2)] + [pass_on(8 + s, 4, 5, s, 1) for s in range(2)]
    across = [pass_on(10, 2, 6, 0, 4), pass_on(11, 4, 6, 1, 2)]
    third = [pass_on(12 + s, 6, 7, s, 1) for s in range(2)]

    stage1(True)
    stage1_emb(0, True)
    valid = jnp.where((plane == PLANES - 1) & (step == STEPS - 1), 0.0, 1.0)

    def own(s):
        arrive(buf.at[0, s, pl.ds(emb, 8)], r1.at[0, s])
        arrive(buf.at[0, s, pl.ds(emb + 8, 8)], r1.at[1, s])
        arrive(buf.at[0, s, pl.ds(0, emb)], r1.at[2, s])
        for c in first[s]:
            c.start()
        prep_rows((s,), valid, emb, width, buf, mid, ll, ld, tp)

    def landed(u, s):
        arrive(buf.at[u, s], rg.at[u, s])

    own(0)

    def stage3(s, start):
        t, m = cur_of[s]
        tn, mn = next_of[s]
        l = lax.rem(step, 2)
        ln = lax.rem(n_frame, 2)
        send(gres.at[s], gemb.at[l], sr.at[2, s], rr.at[2, l], t, m, start)
        send(pres.at[s, 0], prec.at[l, 0], sr.at[0, s], rr.at[0, l], t, m, start)
        send(pres.at[s, 1], prec.at[ln, 1], sr.at[1, s], rr.at[1, ln], tn, mn, start)

    def round_of(n, group, here, size, send_at):
        return [
            pltpu.make_async_remote_copy(
                src_ref=group.at[here], dst_ref=group.at[here], send_sem=sl.at[n, k - 1], recv_sem=rl.at[n, here],
                device_id=send_at(lax.rem(here + k, size)), device_id_type=MESH,
            )
            for k in range(1, size)
        ]

    def gathered(n, group, here, size):
        for k in range(1, size):
            at = lax.rem(here + k, size)
            arrive(group.at[at], rl.at[n, at])

    cols = (emb, width, buf, pc, mid, rhs, rd)
    work = (emb, width, pc, rhs, rd, ll, ld, scs, acc, ge, en)

    @pl.loop(0, 3)
    def _(chip):
        @pl.when(chip == 0)
        def _():
            landed(1, 0)
            stage1_emb(1, True)

        @pl.when(chip == 1)
        def _():
            landed(2, 0)
            across[0].start()
            second[0].start()
            landed(4, 0)
            second[2].start()
            landed(3, 0)

        @pl.when(chip == 2)
        def _():
            landed(5, 0)

        prep_cols(chip, 0, *cols)
        tiles([(0, 2 * chip)], True, *work)

    ent[...] = en[...]
    en[...] = jnp.zeros_like(en)
    own(1)
    landed(6, 0)
    third[0].start()

    @pl.loop(0, 4)
    def _(i):
        @pl.when(i == 1)
        def _():
            landed(7, 0)
            prep_cols(3, 0, *cols)
            ent[...] = ent[...] + 2.0 * en[...]
            en[...] = jnp.zeros_like(en)
            tiles([(0, 6)], True, *work)
            ent[...] = ent[...] + en[...]
            en[...] = jnp.zeros_like(en)
            landed(2, 1)
            second[1].start()
            landed(4, 1)
            across[1].start()
            second[3].start()

        @pl.when(i == 2)
        def _():
            landed(1, 1)
            landed(3, 1)
            prep_cols(0, 1, *cols)
            prep_cols(1, 1, *cols)
            landed(6, 1)
            third[1].start()
            ent[...] = ent[...] + 2.0 * en[...]
            en[...] = jnp.zeros_like(en)

        @pl.when(i == 3)
        def _():
            landed(5, 1)
            prep_cols(2, 1, *cols)
            landed(7, 1)
            prep_cols(3, 1, *cols)

        g = 4 * lax.rem(i, 2) + i // 2
        tiles([(width, g), (width, g + 2)], True, *work)

    l1[track] = ent[...] + en[...]
    finish((1,), weight, emb, width, acc, ge, tp, gres, pres)
    round1 = round_of(0, l1, track, n_track, lambda t: (t, tm))
    round2 = round_of(1, l2, tm, n_tm, lambda m: (track, m))
    for c in round1:
        c.start()
    stage3(1, True)

    @pl.loop(0, 2)
    def _(i):
        @pl.when(i == 1)
        def _():
            gathered(0, l1, track, n_track)
            l2[tm] = jnp.sum(l1[...], axis=0)
            for c in round2:
                c.start()

        tiles([(0, 4 * i + 1), (0, 4 * i + 3)], ENERGY, *work)

    finish((0,), weight, emb, width, acc, ge, tp, gres, pres)
    stage3(0, True)
    for l in range(2):
        arrive(prec.at[l, 0], rr.at[0, l])
        arrive(prec.at[l, 1], rr.at[1, l])
        for c in range(3):
            gpos[c, l : l + 1, :] = prec[l, 0, c : c + 1, :] + prec[l, 1, c : c + 1, :]
        arrive(gemb.at[l], rr.at[2, l])
    gathered(1, l2, tm, n_tm)
    pairs = tracks * (tracks - 1) / 2.0 * (frames - 1)
    total = jnp.sum(jnp.sum(jnp.sum(l2[...], axis=0), axis=0, keepdims=True), axis=1, keepdims=True)
    lout[...] = total * (0.25 / pairs)

    stage1(False)
    stage1_emb(None, False)
    for c in first[0] + first[1] + second + across + third + round1 + round2:
        c.wait_send()
    for s in range(2):
        stage3(s, False)


def on_device(positions, embeddings, visible):
    frames_local, emb, width = embeddings.shape
    tracks = width * lax.axis_size("track")
    frames = frames_local * lax.axis_size("tm")
    R = width
    C = 2 * width
    K = 3 * emb + LANE
    dma, vmem = pltpu.SemaphoreType.DMA, pltpu.VMEM
    scratch = [
        vmem((3, 2, width), f32),
        vmem((2, width), jnp.int32),
        vmem((2, emb, width), f32),
        vmem((2, 8, width), f32),
        dma((3,)),
        vmem((8, 2, emb + 16, width), f32),
        vmem((8, 2, 16, width), f32),
        vmem((16, LANE), f32),
        vmem((8, K, C), bf16),
        vmem((8, 2, 32, C), bf16),
        vmem((C, K), bf16),
        vmem((2, C, 32), bf16),
        vmem((2, C, LANE), f32),
        vmem((8, C, LANE), f32),
        vmem((C, emb), f32),
        vmem((8, LANE), f32),
        vmem((8, LANE), f32),
        vmem((2, emb, width), f32),
        vmem((2, 2, 8, width), f32),
        vmem((2, 2, 8, width), f32),
        vmem((16, 8, LANE), f32),
        vmem((16, 8, LANE), f32),
    ]
    for _ in range(NBUF):
        scratch += [vmem((R, C), f32)] * 3 + [vmem((2 * R, C), bf16)]
    scratch += [dma((3, 2)), dma((3, 2)), dma((8, 2)), dma((14,)), dma((3, 2)), dma((3, 2)), dma((2, 16)), dma((2, 15))]
    whole, there = pl.BlockSpec(memory_space=pltpu.VMEM), pl.BlockSpec(memory_space=pl.ANY)
    grad_pos, grad_emb, loss = pl.pallas_call(
        functools.partial(kernel, R, emb, width, tracks, frames),
        out_shape=[
            vmem((3, 2, width), f32),
            vmem((2, emb, width), f32),
            vmem((1, 1), f32),
        ],
        in_specs=[there] * 3,
        out_specs=[whole] * 3,
        scratch_shapes=scratch,
        compiler_params=pltpu.CompilerParams(
            collective_id=0, has_side_effects=True, vmem_limit_bytes=60 * 2**20
        ),
    )(positions, embeddings, visible)
    return (grad_pos, grad_emb, loss.reshape(()))


def solution(mesh):
    in_specs = (P(None, "tm", "track"), P("tm", None, "track"), P("tm", "track"))
    out_specs = (P(None, "tm", "track"), P("tm", None, "track"), P())
    return jax.shard_map(
        on_device, mesh=mesh, in_specs=in_specs, out_specs=out_specs, check_vma=False
    )
```
